32 devices in a mesh: gz: 8 (over z, y), xy: 4 (over x, core).
Axes of the slice: x: 2, y: 2, z: 4, core: 2. Of those that a mesh axis runs over, the one named last changes fastest.
Arguments:
- volume: float32 [128, 128, 128], P('gz', 'xy'), may hold values from -6 to 6
- owners: int32 [4, 32, 1], P('xy', 'gz'), may hold values from 0 to 7; in each aligned block of 4 rows (0 to 3, 4 to 7, ..., all dimensions but the last counted through in order) at most 2 rows name the same one
Outputs:
- denoised: float32 [128, 128, 128], P('gz', 'xy')
- routed: float32 [4, 128, 128, 128], P('xy', 'gz')
The draws below stay inside these ranges and needn't reach their ends.
Inputs may be any that keep to these rules, and one draw needn't show every extreme that they name: `owners`: among the 4 blocks of one device no destination is named more than 2 times, a bound that some block reaches.
All inputs are finite; a program needn't handle non-finite values.
Results may differ from the reference program's by a relative error of at most 0.0003.
Values sent between devices are 32-bit elements; how exact they have to be, the bound alone decides.
No kernel may reach another device: no remote copies, remote signals or barrier semaphores. Data moves between devices by JAX's collectives and lax.ppermute only.
A program may use at most 64 MiB of HBM per device.

```python
import math
import jax
import jax.numpy as jnp
import numpy as np
from jax import lax

CZ = 16
CY = 32
NX = 128
STEPS = 2
MOST = 2
BLOCK_ROWS = 128
NZ = 128
NY = 128
BLK_DEV = 4
BLOCKS = 32
N_GZ = 8
N_XY = 4


def draw_volume(key, part):
    key_level = jax.random.fold_in(key, 11)
    shape = (NZ, NY, NX)
    return jax.random.uniform(key_level, shape, jnp.float32, -6.0, 6.0)


def deal_out(stream_key, own, number, rows, count, top, limit, skew):
    ranking = jax.random.permutation(stream_key, count)
    heavy_load, ordinary = shares(count, rows * top, limit, skew, True), shares(count, rows * top, limit, skew, False)
    places = jnp.arange(count)

    def named(sizes, turn):
        used = int((sizes > 0).sum())
        fixed = max(1, used // 4)
        moved = fixed + (places - fixed + turn * (used - fixed)) % max(1, count - fixed)
        return jnp.zeros((count,), jnp.int32).at[ranking[jnp.where(places < fixed, places, moved)]].set(jnp.asarray(sizes, jnp.int32))

    sizes = jnp.where(number % 4 == 0, named(heavy_load, number // 4), named(ordinary, number - number // 4 - 1))
    mixed = jax.random.permutation(jax.random.fold_in(own, 3), count)
    source_of, taker = mixed[0:count // 2 * 2:2], mixed[1:count // 2 * 2:2]
    margin = jnp.minimum(sizes[source_of] - 1, limit - sizes[taker]) // 2
    margin = jnp.where((source_of == ranking[0]) | (taker == ranking[0]) | (sizes[taker] == 0), 0, jnp.maximum(margin, 0))
    moved = jax.random.randint(jax.random.fold_in(own, 4), (count // 2,), 0, 1 << 20) % (margin + 1)
    sizes = sizes.at[source_of].add(-moved).at[taker].add(moved)
    labels = jnp.searchsorted(jnp.cumsum(sizes), jnp.arange(rows * top), side="right").astype(jnp.int32)
    table = labels.reshape(top, rows).T
    table = table[jax.random.permutation(jax.random.fold_in(own, 1), rows)]
    turn = jax.random.randint(jax.random.fold_in(own, 2), (rows, 1), 0, top)
    return jnp.take_along_axis(table, (jnp.arange(top)[None, :] + turn) % top, axis=1)


def shares(count, total, bound, skew, full):
    portions = [(1 << 20) // math.isqrt(standing ** skew) + 1 for standing in range(1, count + 1)]
    largest = bound if full else min(bound, max(-(-total // count), total * portions[0] // sum(portions)))
    least = 1 if total - largest >= count - 1 else 0
    given, spare = [largest] + [least] * (count - 1), total - largest - least * (count - 1)
    while spare > 0:
        free = [i for i in range(1, count) if given[i] < largest] or [i for i in range(1, count) if given[i] < bound]
        mass, budget = sum([portions[i] for i in free]), spare
        for i in free:
            extra = min(bound - given[i], max(1, budget * portions[i] // mass), spare)
            given[i] = given[i] + extra
            spare = spare - extra
    return np.array(given)


def setup_inputs(seed: int = 0) -> dict:
    keys = jax.random.split(jax.random.key(seed), 3)
    volume = draw_volume(jax.random.fold_in(keys[2], 71), 0)
    owners_keys = jax.random.split(jax.random.fold_in(keys[1], 1), N_XY * BLOCKS // BLK_DEV)
    owners_turns = jax.random.permutation(jax.random.fold_in(keys[1], 3), N_XY * BLOCKS // BLK_DEV)
    owners = jax.vmap(lambda own, number: deal_out(jax.random.fold_in(keys[1], 2), own, number, BLK_DEV, N_GZ, 1, MOST, 2))(owners_keys, owners_turns).reshape((N_XY, BLOCKS, 1))
    return dict(volume=volume, owners=owners)


TIME_STEP = 30.0
CONTRAST = 4.0


def shifted(field, stride, line_axis, fill, before):
    length = field.shape[line_axis]
    if stride >= length:
        return jnp.full_like(field, fill)
    shape = list(field.shape)
    shape[line_axis] = stride
    padding = jnp.full(tuple(shape), fill, field.dtype)
    if before:
        return jnp.concatenate([padding, lax.slice_in_dim(field, 0, length - stride, axis=line_axis)], axis=line_axis)
    return jnp.concatenate([lax.slice_in_dim(field, stride, length, axis=line_axis), padding], axis=line_axis)


def cyclic_solve(low_diag, main_diag, high_diag, right_side, line_axis, side_axis):
    length = main_diag.shape[line_axis]
    stride = 1
    while stride < length:
        low_prev = shifted(low_diag, stride, line_axis, 0.0, True)
        main_prev = shifted(main_diag, stride, line_axis, 1.0, True)
        high_prev = shifted(high_diag, stride, line_axis, 0.0, True)
        side_prev = shifted(right_side, stride, side_axis, 0.0, True)
        low_next = shifted(low_diag, stride, line_axis, 0.0, False)
        main_next = shifted(main_diag, stride, line_axis, 1.0, False)
        high_next = shifted(high_diag, stride, line_axis, 0.0, False)
        side_next = shifted(right_side, stride, side_axis, 0.0, False)
        factor_low = -low_diag / main_prev
        factor_high = -high_diag / main_next
        main_diag = main_diag + factor_low * high_prev + factor_high * low_next
        right_side = right_side + factor_low * side_prev + factor_high * side_next
        low_diag = factor_low * low_prev
        high_diag = factor_high * high_next
        stride = stride * 2
    return right_side / main_diag


def coefficients(g_line, line_axis, has_before, has_after):
    length = g_line.shape[line_axis] - 2
    weight = 0.5 * (lax.slice_in_dim(g_line, 0, length + 1, axis=line_axis) + lax.slice_in_dim(g_line, 1, length + 2, axis=line_axis))
    shape = [1] * weight.ndim
    shape[line_axis] = length + 1
    edge_index = lax.broadcasted_iota(jnp.int32, tuple(shape), line_axis)
    keep_mask = jnp.where(edge_index == 0, has_before, 1.0) * jnp.where(edge_index == length, has_after, 1.0)
    weight = weight * keep_mask
    low_diag = -3.0 * TIME_STEP * lax.slice_in_dim(weight, 0, length, axis=line_axis)
    high_diag = -3.0 * TIME_STEP * lax.slice_in_dim(weight, 1, length + 1, axis=line_axis)
    main_diag = 1.0 - low_diag - high_diag
    return low_diag, main_diag, high_diag


def pad_zero(field, line_axis):
    widths = [(0, 0)] * field.ndim
    widths[line_axis] = (1, 1)
    return jnp.pad(field, widths)


def diffusivity(field):
    squares = None
    for line_axis in range(3):
        length = field.shape[line_axis]
        later = jnp.concatenate([lax.slice_in_dim(field, 1, length, axis=line_axis), lax.slice_in_dim(field, length - 1, length, axis=line_axis)], axis=line_axis)
        earlier = jnp.concatenate([lax.slice_in_dim(field, 0, 1, axis=line_axis), lax.slice_in_dim(field, 0, length - 1, axis=line_axis)], axis=line_axis)
        slope = (later - earlier) * 0.5
        squares = slope * slope if squares is None else squares + slope * slope
    return 1.0 / (1.0 + squares / CONTRAST)


def line_solve(g_field, right_side, line_axis):
    low_diag, main_diag, high_diag = coefficients(pad_zero(g_field, line_axis), line_axis, 0.0, 0.0)
    return cyclic_solve(low_diag, main_diag, high_diag, right_side, line_axis, line_axis)


def reference(volume, owners):
    field = volume
    for section_index in range(STEPS):
        g_field = diffusivity(field)
        along_x = line_solve(g_field, field, 2)
        along_y = line_solve(g_field, field, 1)
        along_z = line_solve(g_field, field, 0)
        field = (along_x + along_y + along_z) / 3.0
    blocks_all = field.reshape(N_GZ, CZ, N_XY, CY, NX).transpose(2, 0, 1, 3, 4).reshape(N_XY, N_GZ, BLK_DEV, BLOCK_ROWS, NX)
    targets = owners[:, :, 0].reshape(N_XY, N_GZ, BLK_DEV)
    same = targets[..., :, None] == targets[..., None, :]
    block_iota = jnp.arange(BLK_DEV, dtype=jnp.int32)
    earlier = block_iota[:, None] < block_iota[None, :]
    order_rank = jnp.sum((same & earlier).astype(jnp.int32), axis=-2)
    source_iota = jnp.arange(N_GZ, dtype=jnp.int32).reshape(1, N_GZ, 1)
    slot_index = targets * (N_GZ * MOST) + source_iota * MOST + order_rank
    column_iota = jnp.arange(N_XY, dtype=jnp.int32).reshape(N_XY, 1, 1)
    routed = jnp.zeros((N_XY, N_GZ * N_GZ * MOST, BLOCK_ROWS, NX), field.dtype)
    routed = routed.at[column_iota, slot_index].set(blocks_all)
    return field, routed
```

```python
import functools

import jax
import jax.numpy as jnp
from jax import lax
from jax.experimental import pallas as pl
from jax.experimental.pallas import tpu as pltpu
from jax.sharding import PartitionSpec as P

STEPS = 2
MOST = 2
BLOCK_ROWS = 128
TIME_STEP = 30.0
CONTRAST = 4.0
HALF_LINK = 1.5 * TIME_STEP
THIRD = 1.0 / 3.0
VMEM = pltpu.VMEM


def call(body, outs, ins, name, smem=()):
    specs = [
        pl.BlockSpec(memory_space=pltpu.SMEM if k in smem else VMEM) for k in range(len(ins))
    ]
    return pl.pallas_call(
        body,
        out_shape=[jax.ShapeDtypeStruct(shape, jnp.float32) for shape in outs],
        in_specs=specs,
        out_specs=[pl.BlockSpec(memory_space=VMEM)] * len(outs),
        name=name,
    )(*ins)


def facing(index, low, high):
    odd = lax.rem(index, 2) == 1
    return jnp.where(odd, low, high), jnp.where(odd, high, low)


def edge_kernel(depth, height, field, z_first, z_second, y_first, y_second):
    z_odd = lax.rem(lax.axis_index("gz"), 2) == 1
    y_odd = lax.rem(lax.axis_index("xy"), 2) == 1
    bottom, top = field[pl.ds(0, height), :], field[pl.ds((depth - 1) * height, height), :]
    z_first[...] = jnp.where(z_odd, bottom, top)
    z_second[...] = jnp.where(z_odd, top, bottom)
    near = field[pl.ds(0, depth, stride=height), :]
    far = field[pl.ds(height - 1, depth, stride=height), :]
    y_first[...] = jnp.where(y_odd, near, far)
    y_second[...] = jnp.where(y_odd, far, near)


def chain(g_rows, v_rows, count, solved, head, tail, element):
    g_head = g_prev = g_rows(0)
    pivot = jnp.ones_like(g_prev)
    right = v_rows(0)
    unit = pivot
    for k in range(count - 1):
        g_next = g_rows(k + 1)
        link = HALF_LINK * (g_prev + g_next)
        inverse = 1.0 / (pivot + link)
        ratio = link * inverse
        solved[k] = right * inverse
        head[k] = unit * inverse
        tail[k] = ratio
        pivot = 1.0 + ratio * pivot
        right = v_rows(k + 1) + ratio * right
        unit = ratio * unit
        g_prev = g_next
    inverse = 1.0 / pivot
    value, from_head, from_tail = right * inverse, unit * inverse, inverse
    solved[count - 1] = value
    head[count - 1] = from_head
    tail[count - 1] = from_tail
    element[2] = from_tail
    element[4] = value
    element[5] = g_head
    element[6] = g_prev
    for k in range(count - 2, -1, -1):
        ratio = tail[k]
        value = solved[k] + ratio * value
        from_head = head[k] + ratio * from_head
        from_tail = ratio * from_tail
        solved[k] = value
        head[k] = from_head
        tail[k] = from_tail
    element[0] = from_head
    element[1] = from_tail
    element[3] = value


def z_kernel(depth, height, late, *refs):
    if late:
        field, z_first, z_second, y_first, y_second, z_low, z_high = refs[:7]
    else:
        field, z_first, z_second, y_first, y_second = refs[:5]
    g_out, solved, head, tail, element = refs[-5:]
    z_index, y_index = lax.axis_index("gz"), lax.axis_index("xy")
    z_odd, y_odd = lax.rem(z_index, 2) == 1, lax.rem(y_index, 2) == 1
    plane = lambda k: field[pl.ds(k * height, height), :]
    first, second = z_first[...], z_second[...]
    low, high = jnp.where(z_odd, first, second), jnp.where(z_odd, second, first)
    if late:
        low, high = (low + z_low[...]) * THIRD, (high + z_high[...]) * THIRD
    low = jnp.where(z_index == 0, plane(0), low)
    high = jnp.where(z_index == lax.axis_size("gz") - 1, plane(depth - 1), high)
    width = field.shape[1]
    rows = lax.broadcasted_iota(jnp.int32, (height, width), 0)
    lanes = lax.broadcasted_iota(jnp.int32, (height, width), 1)
    y_begin, y_end = y_index == 0, y_index == lax.axis_size("xy") - 1

    def g_rows(k):
        here = plane(k)
        slope = (plane(k + 1) if k < depth - 1 else high) - (plane(k - 1) if k else low)
        squares = (slope * 0.5) * (slope * 0.5)
        one, two = y_first[pl.ds(k, 1), :], y_second[pl.ds(k, 1), :]
        near, far = jnp.where(y_odd, one, two), jnp.where(y_odd, two, one)
        near = jnp.where(y_begin, here[:1], near)
        far = jnp.where(y_end, here[height - 1 :], far)
        after = jnp.where(rows == height - 1, far, pltpu.roll(here, height - 1, 0))
        before = jnp.where(rows == 0, near, pltpu.roll(here, 1, 0))
        slope = (after - before) * 0.5
        squares = squares + slope * slope
        after = jnp.where(lanes == width - 1, here, pltpu.roll(here, width - 1, 1))
        before = jnp.where(lanes == 0, here, pltpu.roll(here, 1, 1))
        slope = (after - before) * 0.5
        squares = squares + slope * slope
        g = 1.0 / (1.0 + squares * (1.0 / CONTRAST))
        g_out[pl.ds(k * height, height), :] = g
        return g

    chain(g_rows, plane, depth, solved, head, tail, element)


def y_kernel(depth, height, g_field, field, solved, head, tail, element):
    g_rows = lambda k: g_field[pl.ds(k, depth, stride=height), :]
    v_rows = lambda k: field[pl.ds(k, depth, stride=height), :]
    chain(g_rows, v_rows, height, solved, head, tail, element)


def x_kernel(rows, g_field, field, solved):
    width = field.shape[1]
    lanes = lax.broadcasted_iota(jnp.int32, (rows, width), 1)

    def piece(step, carry):
        at = pl.ds(pl.multiple_of(step * rows, rows), rows)
        g = g_field[at, :]
        right = field[at, :]
        link = jnp.where(
            lanes == width - 1, 0.0, HALF_LINK * (g + pltpu.roll(g, width - 1, 1))
        )
        main = 1.0 + link + pltpu.roll(link, 1, 1)
        stride = 1
        while stride < width:
            inverse = 1.0 / main
            factor = link * inverse
            back = width - stride
            ahead = link * pltpu.roll(inverse, back, 1)
            main = main - pltpu.roll(link * factor, stride, 1) - link * ahead
            right = right + pltpu.roll(factor * right, stride, 1) + ahead * pltpu.roll(right, back, 1)
            link = ahead * pltpu.roll(link, back, 1)
            stride *= 2
        solved[at, :] = right / main
        return carry

    lax.fori_loop(0, field.shape[0] // rows, piece, 0)


def sum_kernel(depth, height, along_x, solved, head, tail, from_low, from_high, total, z_first, z_second):
    low, high = from_low[...], from_high[...]
    for k in range(height):
        at = pl.ds(k, depth, stride=height)
        total[at, :] = along_x[at, :] + (solved[k] + low * head[k] + high * tail[k])
    z_odd = lax.rem(lax.axis_index("gz"), 2) == 1
    bottom, top = total[pl.ds(0, height), :], total[pl.ds((depth - 1) * height, height), :]
    z_first[...] = jnp.where(z_odd, bottom, top)
    z_second[...] = jnp.where(z_odd, top, bottom)


def step_kernel(depth, height, total, solved, head, tail, from_low, from_high, jump_low, jump_high,
                field, y_first, y_second, z_low, z_high):
    low, high = from_low[...], from_high[...]
    for k in range(depth):
        at = pl.ds(k * height, height)
        along_z = solved[k] + low * head[k] + high * tail[k]
        if k == 0:
            z_low[...] = along_z + jump_low[...]
        if k == depth - 1:
            z_high[...] = along_z - jump_high[...]
        field[at, :] = (total[at, :] + along_z) * THIRD
    y_odd = lax.rem(lax.axis_index("xy"), 2) == 1
    near = field[pl.ds(0, depth, stride=height), :]
    far = field[pl.ds(height - 1, depth, stride=height), :]
    y_first[...] = jnp.where(y_odd, near, far)
    y_second[...] = jnp.where(y_odd, far, near)


def last_kernel(depth, height, total, solved, head, tail, from_low, from_high, owners, field, outgoing):
    low, high = from_low[...], from_high[...]
    outgoing[...] = jnp.zeros_like(outgoing)
    planes = BLOCK_ROWS // height
    for block in range(depth // planes):
        owner = owners[0, block]
        rank = jnp.int32(0)
        for other in range(block):
            rank = rank + (owners[0, other] == owner).astype(jnp.int32)
        slot = owner * MOST + rank
        for j in range(planes):
            k = block * planes + j
            at = pl.ds(k * height, height)
            value = (total[at, :] + (solved[k] + low * head[k] + high * tail[k])) * THIRD
            field[at, :] = value
            outgoing[slot, pl.ds(j * height, height), :] = value


def swap(values, axis, stride):
    count = lax.axis_size(axis)
    return lax.ppermute(values, axis, [(i, i ^ stride) for i in range(count)])


def neighbours(first, second, axis):
    count = lax.axis_size(axis)
    other = [(i, i + 1) for i in range(1, count - 1, 2)]
    return swap(first, axis, 1), lax.ppermute(second, axis, other + [(j, i) for i, j in other])


def flows(element, axis):
    index, count = lax.axis_index(axis), lax.axis_size(axis)
    own = [element[k] for k in range(7)]
    zero = jnp.zeros_like(own[0])
    levels = []
    stride = 1
    while stride < count:
        upper = (index // stride) % 2 == 1
        pick = lambda a, b: jnp.where(upper, a, b)
        if stride * 2 < count:
            got = swap(element, axis, stride)
            left = [pick(got[k], own[k]) for k in range(7)]
            right = [pick(own[k], got[k]) for k in range(7)]
        else:
            sent = jnp.stack([pick(own[0], own[2]), pick(own[3], own[4]), pick(own[5], own[6])])
            got = swap(sent, axis, stride)
            left = [None, zero, pick(got[0], own[2]), None, pick(got[1], own[4]), None, pick(got[2], own[6])]
            right = [pick(own[0], got[0]), zero, None, pick(own[3], got[1]), None, pick(own[5], got[2]), None]
        link = HALF_LINK * (left[6] + right[5])
        inverse = 1.0 / (1.0 + link * (left[2] + right[0]))
        gap = left[4] - right[3]
        levels.append((upper, link, inverse, gap, left[1], right[1]))
        stride *= 2
        if stride < count:
            share = link * inverse
            first, second = share * left[1], share * right[1]
            own = [
                left[0] - first * left[1],
                first * right[1],
                right[2] - second * right[1],
                left[3] - first * gap,
                right[4] + second * gap,
                left[5],
                right[6],
            ]
            element = jnp.stack(own)
    from_low = from_high = jump_low = jump_high = zero
    for upper, link, inverse, gap, before, after in reversed(levels):
        jump = (gap + before * from_low - after * from_high) * inverse
        flow = link * jump
        from_low, jump_low = jnp.where(upper, flow, from_low), jnp.where(upper, jump, jump_low)
        from_high, jump_high = jnp.where(upper, from_high, -flow), jnp.where(upper, jump_high, jump)
    return from_low, from_high, jump_low, jump_high


def on_device(volume, owners):
    depth, height, width = volume.shape
    z_count = lax.axis_size("gz")
    flat, plane, side = (depth * height, width), (height, width), (depth, width)
    z_parts, y_parts = (depth, height, width), (height, depth, width)
    part = functools.partial
    field = volume.reshape(flat)
    edges = call(part(edge_kernel, depth, height), [plane, plane, side, side], [field], "edges")
    z_sides, y_sides = neighbours(*edges[:2], "gz"), neighbours(*edges[2:], "xy")
    ghosts = ()
    for step in range(STEPS):
        g_field, z_solved, z_head, z_tail, z_element = call(
            part(z_kernel, depth, height, step > 0),
            [flat, z_parts, z_parts, z_parts, (7,) + plane],
            [field, *z_sides, *y_sides, *ghosts],
            "z_pieces",
        )
        z_low, z_high, jump_low, jump_high = flows(z_element, "gz")
        y_solved, y_head, y_tail, y_element = call(
            part(y_kernel, depth, height),
            [y_parts, y_parts, y_parts, (7,) + side],
            [g_field, field],
            "y_pieces",
        )
        y_low, y_high, _, _ = flows(y_element, "xy")
        (along_x,) = call(part(x_kernel, 64), [flat], [g_field, field], "x_lines")
        total, *z_edges = call(
            part(sum_kernel, depth, height),
            [flat, plane, plane],
            [along_x, y_solved, y_head, y_tail, y_low, y_high],
            "sum_xy",
        )
        if step < STEPS - 1:
            z_sides = neighbours(*z_edges, "gz")
            field, *rest = call(
                part(step_kernel, depth, height),
                [flat, side, side, plane, plane],
                [total, z_solved, z_head, z_tail, z_low, z_high, jump_low, jump_high],
                "new_field",
            )
            y_sides, ghosts = neighbours(*rest[:2], "xy"), rest[2:]
    blocks = owners.shape[1]
    field, outgoing = call(
        part(last_kernel, depth, height),
        [flat, (z_count * MOST, BLOCK_ROWS, width)],
        [total, z_solved, z_head, z_tail, z_low, z_high, owners.reshape(1, blocks)],
        "denoised",
        smem=(6,),
    )
    incoming = lax.all_to_all(outgoing, "gz", split_axis=0, concat_axis=0, tiled=True)
    return field.reshape(volume.shape), incoming.reshape(1, z_count * MOST, BLOCK_ROWS, width)


def solution(mesh):
    in_specs = (P("gz", "xy", None), P("xy", "gz", None))
    out_specs = (P("gz", "xy", None), P("xy", "gz", None, None))
    return jax.shard_map(
        on_device, mesh=mesh, in_specs=in_specs, out_specs=out_specs, check_vma=False
    )
```

```python
import functools

import jax
import jax.numpy as jnp
from jax import lax
from jax.experimental import pallas as pl
from jax.experimental.pallas import tpu as pltpu
from jax.sharding import PartitionSpec as P

STEPS = 2
MOST = 2
BLOCK_ROWS = 128
TIME_STEP = 30.0
CONTRAST = 4.0
HALF_LINK = 1.5 * TIME_STEP
THIRD = 1.0 / 3.0
VMEM_LIMIT = 16 * 1024 * 1024
VMEM = pltpu.VMEM


def call(body, outs, ins, name, smem=(), after=()):
    count = len(ins)
    specs = [
        pl.BlockSpec(memory_space=pltpu.SMEM if k in smem else VMEM) for k in range(count)
    ] + [pl.BlockSpec(memory_space=pl.ANY)] * len(after)
    return pl.pallas_call(
        lambda *refs: body(*refs[:count], *refs[count + len(after) :]),
        out_shape=[jax.ShapeDtypeStruct(shape, jnp.float32) for shape in outs],
        in_specs=specs,
        out_specs=[pl.BlockSpec(memory_space=VMEM)] * len(outs),
        compiler_params=pltpu.CompilerParams(vmem_limit_bytes=VMEM_LIMIT),
        name=name,
    )(*ins, *after)


def edge_kernel(depth, height, owners, field, z_first, z_second, y_first, y_second, slots):
    z_odd = lax.rem(lax.axis_index("gz"), 2) == 1
    y_odd = lax.rem(lax.axis_index("xy"), 2) == 1
    bottom, top = field[pl.ds(0, height), :], field[pl.ds((depth - 1) * height, height), :]
    z_first[...] = jnp.where(z_odd, bottom, top)
    z_second[...] = jnp.where(z_odd, top, bottom)
    near = field[pl.ds(0, depth, stride=height), :]
    far = field[pl.ds(height - 1, depth, stride=height), :]
    y_first[...] = jnp.where(y_odd, near, far)
    y_second[...] = jnp.where(y_odd, far, near)
    for block in range(slots.shape[0]):
        rank = jnp.int32(0)
        for other in range(block):
            rank = rank + (owners[0, other] == owners[0, block]).astype(jnp.int32)
        slot = owners[0, block] * MOST + rank
        slots[pl.ds(block, 1), :] = jnp.full((1, slots.shape[1]), slot.astype(jnp.float32))


def chain(g_rows, v_rows, count, solved, head, tail, element):
    g_head = g_prev = g_rows(0)
    pivot = jnp.ones_like(g_prev)
    right = v_rows(0)
    unit = pivot
    for k in range(count - 1):
        g_next = g_rows(k + 1)
        link = HALF_LINK * (g_prev + g_next)
        inverse = 1.0 / (pivot + link)
        ratio = link * inverse
        solved[k] = right * inverse
        head[k] = unit * inverse
        tail[k] = ratio
        pivot = 1.0 + ratio * pivot
        right = v_rows(k + 1) + ratio * right
        unit = ratio * unit
        g_prev = g_next
    inverse = 1.0 / pivot
    value, from_head, from_tail = right * inverse, unit * inverse, inverse
    solved[count - 1] = value
    head[count - 1] = from_head
    tail[count - 1] = from_tail
    element[2] = from_tail
    element[4] = value
    element[5] = g_head
    element[6] = g_prev
    for k in range(count - 2, -1, -1):
        ratio = tail[k]
        value = solved[k] + ratio * value
        from_head = head[k] + ratio * from_head
        from_tail = ratio * from_tail
        solved[k] = value
        head[k] = from_head
        tail[k] = from_tail
    element[0] = from_head
    element[1] = from_tail
    element[3] = value


def z_kernel(depth, height, late, *refs):
    if late:
        field, z_first, z_second, y_first, y_second, z_low, z_high = refs[:7]
    else:
        field, z_first, z_second, y_first, y_second = refs[:5]
    g_out, solved, head, tail, element = refs[-5:]
    z_index, y_index = lax.axis_index("gz"), lax.axis_index("xy")
    z_odd, y_odd = lax.rem(z_index, 2) == 1, lax.rem(y_index, 2) == 1
    plane = lambda k: field[pl.ds(k * height, height), :]
    first, second = z_first[...], z_second[...]
    low, high = jnp.where(z_odd, first, second), jnp.where(z_odd, second, first)
    if late:
        low, high = (low + z_low[...]) * THIRD, (high + z_high[...]) * THIRD
    low = jnp.where(z_index == 0, plane(0), low)
    high = jnp.where(z_index == lax.axis_size("gz") - 1, plane(depth - 1), high)
    width = field.shape[1]
    rows = lax.broadcasted_iota(jnp.int32, (height, width), 0)
    lanes = lax.broadcasted_iota(jnp.int32, (height, width), 1)
    y_begin, y_end = y_index == 0, y_index == lax.axis_size("xy") - 1

    def g_rows(k):
        here = plane(k)
        slope = (plane(k + 1) if k < depth - 1 else high) - (plane(k - 1) if k else low)
        squares = (slope * 0.5) * (slope * 0.5)
        one, two = y_first[pl.ds(k, 1), :], y_second[pl.ds(k, 1), :]
        near, far = jnp.where(y_odd, one, two), jnp.where(y_odd, two, one)
        near = jnp.where(y_begin, here[:1], near)
        far = jnp.where(y_end, here[height - 1 :], far)
        after = jnp.where(rows == height - 1, far, pltpu.roll(here, height - 1, 0))
        before = jnp.where(rows == 0, near, pltpu.roll(here, 1, 0))
        slope = (after - before) * 0.5
        squares = squares + slope * slope
        after = jnp.where(lanes == width - 1, here, pltpu.roll(here, width - 1, 1))
        before = jnp.where(lanes == 0, here, pltpu.roll(here, 1, 1))
        slope = (after - before) * 0.5
        squares = squares + slope * slope
        g = 1.0 / (1.0 + squares * (1.0 / CONTRAST))
        g_out[pl.ds(k * height, height), :] = g
        return g

    chain(g_rows, plane, depth, solved, head, tail, element)


def y_kernel(depth, height, g_field, field, solved, head, tail, element):
    g_rows = lambda k: g_field[pl.ds(k, depth, stride=height), :]
    v_rows = lambda k: field[pl.ds(k, depth, stride=height), :]
    chain(g_rows, v_rows, height, solved, head, tail, element)


def x_kernel(rows, g_field, field, solved):
    width = field.shape[1]
    lanes = lax.broadcasted_iota(jnp.int32, (rows, width), 1)

    def piece(step, carry):
        at = pl.ds(pl.multiple_of(step * rows, rows), rows)
        g = g_field[at, :]
        right = field[at, :]
        link = jnp.where(
            lanes == width - 1, 0.0, HALF_LINK * (g + pltpu.roll(g, width - 1, 1))
        )
        main = 1.0 + link + pltpu.roll(link, 1, 1)
        stride = 1
        while stride < width:
            inverse = 1.0 / main
            factor = link * inverse
            back = width - stride
            ahead = link * pltpu.roll(inverse, back, 1)
            main = main - pltpu.roll(link * factor, stride, 1) - link * ahead
            right = right + pltpu.roll(factor * right, stride, 1) + ahead * pltpu.roll(right, back, 1)
            link = ahead * pltpu.roll(link, back, 1)
            stride *= 2
        solved[at, :] = right / main
        return carry

    lax.fori_loop(0, field.shape[0] // rows, piece, 0)


def join(lower, upper_piece):
    link = HALF_LINK * (lower[6] + upper_piece[5])
    inverse = 1.0 / (1.0 + link * (lower[2] + upper_piece[0]))
    return link, inverse, lower[4] - upper_piece[3]


def sides(upper, own, got, last):
    pick = lambda a, b: jnp.where(upper, a, b)
    if not last:
        return [pick(got[k], own[k]) for k in range(7)], [pick(own[k], got[k]) for k in range(7)]
    zero = jnp.zeros_like(own[0])
    lower = [None, zero, pick(got[0], own[2]), None, pick(got[1], own[4]), None, pick(got[2], own[6])]
    return lower, [pick(own[0], got[0]), zero, None, pick(own[3], got[1]), None, pick(own[5], got[2]), None]


def is_upper(axis, level):
    return lax.rem(lax.div(lax.axis_index(axis), 1 << level), 2) == 1


def merge_kernel(axis, level, own, got, *outs):
    upper = is_upper(axis, level)
    lower, higher = sides(upper, own, got, False)
    link, inverse, gap = join(lower, higher)
    share = link * inverse
    first, second = share * lower[1], share * higher[1]
    merged = [
        lower[0] - first * lower[1],
        first * higher[1],
        higher[2] - second * higher[1],
        lower[3] - first * gap,
        higher[4] + second * gap,
        lower[5],
        higher[6],
    ]
    for k in range(7):
        outs[0][k] = merged[k]
    if len(outs) > 1:
        above = is_upper(axis, level + 1)
        for k, (high, low) in enumerate(((0, 2), (3, 4), (5, 6))):
            outs[1][k] = jnp.where(above, merged[high], merged[low])


def unwind(axis, pairs):
    zero = jnp.zeros_like(pairs[0][0])
    from_low = from_high = jump_low = jump_high = zero
    for level in range(len(pairs) // 2 - 1, -1, -1):
        upper = is_upper(axis, level)
        own, got = pairs[2 * level], pairs[2 * level + 1]
        lower, higher = sides(upper, own, got, level == len(pairs) // 2 - 1)
        link, inverse, gap = join(lower, higher)
        jump = (gap + lower[1] * from_low - higher[1] * from_high) * inverse
        flow = link * jump
        from_low, jump_low = jnp.where(upper, flow, from_low), jnp.where(upper, jump, jump_low)
        from_high, jump_high = jnp.where(upper, from_high, -flow), jnp.where(upper, jump_high, jump)
    return from_low, from_high, jump_low, jump_high


def sum_kernel(depth, height, edges, along_x, solved, head, tail, *refs):
    pairs, outs = refs[: len(refs) - 1 - 2 * edges], refs[len(refs) - 1 - 2 * edges :]
    total = outs[0]
    low, high, _, _ = unwind("xy", [[ref[k] for k in range(ref.shape[0])] for ref in pairs])
    for k in range(height):
        at = pl.ds(k, depth, stride=height)
        total[at, :] = along_x[at, :] + (solved[k] + low * head[k] + high * tail[k])
    if edges:
        z_odd = lax.rem(lax.axis_index("gz"), 2) == 1
        bottom, top = total[pl.ds(0, height), :], total[pl.ds((depth - 1) * height, height), :]
        outs[1][...] = jnp.where(z_odd, bottom, top)
        outs[2][...] = jnp.where(z_odd, top, bottom)


def step_kernel(depth, height, total, solved, head, tail, *refs):
    field, y_first, y_second, z_low, z_high = refs[-5:]
    low, high, jump_low, jump_high = unwind("gz", [[ref[k] for k in range(ref.shape[0])] for ref in refs[:-5]])
    for k in range(depth):
        at = pl.ds(k * height, height)
        along_z = solved[k] + low * head[k] + high * tail[k]
        if k == 0:
            z_low[...] = along_z + jump_low
        if k == depth - 1:
            z_high[...] = along_z - jump_high
        field[at, :] = (total[at, :] + along_z) * THIRD
    y_odd = lax.rem(lax.axis_index("xy"), 2) == 1
    near = field[pl.ds(0, depth, stride=height), :]
    far = field[pl.ds(height - 1, depth, stride=height), :]
    y_first[...] = jnp.where(y_odd, near, far)
    y_second[...] = jnp.where(y_odd, far, near)


def last_kernel(depth, height, slots, total, solved, head, tail, *refs):
    field, outgoing = refs[-2:]
    low, high, _, _ = unwind("gz", [[ref[k] for k in range(ref.shape[0])] for ref in refs[:-2]])
    outgoing[...] = jnp.zeros_like(outgoing)
    planes = BLOCK_ROWS // height
    for block in range(depth // planes):
        slot = jnp.max(slots[pl.ds(block, 1), :]).astype(jnp.int32)
        for j in range(planes):
            k = block * planes + j
            at = pl.ds(k * height, height)
            value = (total[at, :] + (solved[k] + low * head[k] + high * tail[k])) * THIRD
            field[at, :] = value
            outgoing[slot, pl.ds(j * height, height), :] = value


def swap(values, axis, stride):
    count = lax.axis_size(axis)
    return lax.ppermute(values, axis, [(i, i ^ stride) for i in range(count)])


def neighbours(first, second, axis):
    count = lax.axis_size(axis)
    other = [(i, (i + 1) % count) for i in range(1, count, 2)]
    return swap(first, axis, 1), lax.ppermute(second, axis, other + [(j, i) for i, j in other])


def merge(element, got, axis, level, after=()):
    shape = element.shape[1:]
    outs = [(7,) + shape] + [(3,) + shape] * (4 << level >= lax.axis_size(axis))
    merged = call(
        functools.partial(merge_kernel, axis, level), outs, [element, got], f"merge_{axis}_{level}", after=after
    )
    return merged[0], merged[-1]


def on_device(volume, owners):
    depth, height, width = volume.shape
    z_count, y_count = lax.axis_size("gz"), lax.axis_size("xy")
    z_rounds, y_rounds = z_count.bit_length() - 1, y_count.bit_length() - 1
    blocks = owners.shape[1]
    flat, plane, side = (depth * height, width), (height, width), (depth, width)
    z_parts, y_parts = (depth, height, width), (height, depth, width)
    part = functools.partial
    field = volume.reshape(flat)
    *edges, slots = call(
        part(edge_kernel, depth, height),
        [plane, plane, side, side, (blocks, width)],
        [owners.reshape(1, blocks), field],
        "edges",
        smem=(0,),
    )
    z_sides, y_sides = neighbours(*edges[:2], "gz"), neighbours(*edges[2:], "xy")
    ghosts = ()
    for step in range(STEPS):
        last = step == STEPS - 1
        g_field, *z_pieces, z_element = call(
            part(z_kernel, depth, height, step > 0),
            [flat, z_parts, z_parts, z_parts, (7,) + plane],
            [field, *z_sides, *y_sides, *ghosts],
            "z_pieces",
        )
        *y_pieces, y_element = call(
            part(y_kernel, depth, height),
            [y_parts, y_parts, y_parts, (7,) + side],
            [g_field, field],
            "y_pieces",
            after=[z_element],
        )
        y_sent, y_pairs = y_element, []
        z_sent, z_pairs = z_element, []
        for level in range(y_rounds):
            y_pairs += [y_element, swap(y_sent, "xy", 1 << level)]
            if level + 1 < y_rounds:
                y_element, y_sent = merge(*y_pairs[-2:], "xy", level)
        for level in range(z_rounds):
            z_pairs += [z_element, swap(z_sent, "gz", 1 << level)]
            behind = [y_element] if level == 0 else []
            if level == 1:
                (along_x,) = call(
                    part(x_kernel, depth * height), [flat], [g_field, field], "x_lines", after=[z_element]
                )
                total, *z_edges = call(
                    part(sum_kernel, depth, height, not last),
                    [flat] + [plane, plane] * (not last),
                    [along_x, *y_pieces, *y_pairs],
                    "sum_xy",
                )
                behind = [total]
            if level + 1 < z_rounds:
                z_element, z_sent = merge(*z_pairs[-2:], "gz", level, behind)
        if not last:
            z_sides = neighbours(*z_edges, "gz")
            field, *rest = call(
                part(step_kernel, depth, height),
                [flat, side, side, plane, plane],
                [total, *z_pieces, *z_pairs],
                "new_field",
            )
            y_sides, ghosts = neighbours(*rest[:2], "xy"), rest[2:]
    field, outgoing = call(
        part(last_kernel, depth, height),
        [flat, (z_count * MOST, BLOCK_ROWS, width)],
        [slots, total, *z_pieces, *z_pairs],
        "denoised",
    )
    incoming = lax.all_to_all(outgoing, "gz", split_axis=0, concat_axis=0, tiled=True)
    return field.reshape(volume.shape), incoming.reshape(1, z_count * MOST, BLOCK_ROWS, width)


def solution(mesh):
    in_specs = (P("gz", "xy", None), P("xy", "gz", None))
    out_specs = (P("gz", "xy", None), P("xy", "gz", None, None))
    return jax.shard_map(
        on_device, mesh=mesh, in_specs=in_specs, out_specs=out_specs, check_vma=False
    )
```

```python
import functools

import jax
import jax.numpy as jnp
from jax import lax
from jax.experimental import pallas as pl
from jax.experimental.pallas import tpu as pltpu
from jax.sharding import PartitionSpec as P

STEPS = 2
MOST = 2
CHUNKS = 2
BLOCK_ROWS = 128
TIME_STEP = 30.0
CONTRAST = 4.0
HALF_LINK = 1.5 * TIME_STEP
THIRD = 1.0 / 3.0
VMEM_LIMIT = 16 * 1024 * 1024
VMEM = pltpu.VMEM


def call(body, outs, ins, name, smem=(), after=()):
    count = len(ins)
    specs = [
        pl.BlockSpec(memory_space=pltpu.SMEM if k in smem else VMEM) for k in range(count)
    ] + [pl.BlockSpec(memory_space=pl.ANY)] * len(after)
    return pl.pallas_call(
        lambda *refs: body(*refs[:count], *refs[count + len(after) :]),
        out_shape=[jax.ShapeDtypeStruct(shape, jnp.float32) for shape in outs],
        in_specs=specs,
        out_specs=[pl.BlockSpec(memory_space=VMEM)] * len(outs),
        compiler_params=pltpu.CompilerParams(vmem_limit_bytes=VMEM_LIMIT),
        name=name,
    )(*ins, *after)


def edge_kernel(depth, height, field, z_first, z_second, y_first, y_second):
    z_odd = lax.rem(lax.axis_index("gz"), 2) == 1
    y_odd = lax.rem(lax.axis_index("xy"), 2) == 1
    bottom, top = field[pl.ds(0, height), :], field[pl.ds((depth - 1) * height, height), :]
    z_first[...] = jnp.where(z_odd, bottom, top)
    z_second[...] = jnp.where(z_odd, top, bottom)
    near = field[pl.ds(0, depth, stride=height), :]
    far = field[pl.ds(height - 1, depth, stride=height), :]
    y_first[...] = jnp.where(y_odd, near, far)
    y_second[...] = jnp.where(y_odd, far, near)


def slot_kernel(owners, slots):
    slots[...] = jnp.zeros_like(slots)
    for block in range(owners.shape[1]):
        rank = jnp.int32(0)
        for other in range(block):
            rank = rank + (owners[0, other] == owners[0, block]).astype(jnp.int32)
        slot = owners[0, block] * MOST + rank
        slots[pl.ds(block, 1), :] = jnp.full((1, slots.shape[1]), slot.astype(jnp.float32))


def chain(g_rows, v_rows, count, solved, head, tail, element):
    g_head = g_prev = g_rows(0)
    pivot = jnp.ones_like(g_prev)
    right = v_rows(0)
    unit = pivot
    for k in range(count - 1):
        g_next = g_rows(k + 1)
        link = HALF_LINK * (g_prev + g_next)
        inverse = 1.0 / (pivot + link)
        ratio = link * inverse
        solved[k] = right * inverse
        head[k] = unit * inverse
        tail[k] = ratio
        pivot = 1.0 + ratio * pivot
        right = v_rows(k + 1) + ratio * right
        unit = ratio * unit
        g_prev = g_next
    inverse = 1.0 / pivot
    value, from_head, from_tail = right * inverse, unit * inverse, inverse
    solved[count - 1] = value
    head[count - 1] = from_head
    tail[count - 1] = from_tail
    element[2] = from_tail
    element[4] = value
    element[5] = g_head
    element[6] = g_prev
    for k in range(count - 2, -1, -1):
        ratio = tail[k]
        value = solved[k] + ratio * value
        from_head = head[k] + ratio * from_head
        from_tail = ratio * from_tail
        solved[k] = value
        head[k] = from_head
        tail[k] = from_tail
    element[0] = from_head
    element[1] = from_tail
    element[3] = value


def z_kernel(depth, height, late, *refs):
    if late:
        field, z_first, z_second, y_first, y_second, z_low, z_high = refs[:7]
    else:
        field, z_first, z_second, y_first, y_second = refs[:5]
    g_out, solved, head, tail, element = refs[-5:]
    z_index, y_index = lax.axis_index("gz"), lax.axis_index("xy")
    z_odd, y_odd = lax.rem(z_index, 2) == 1, lax.rem(y_index, 2) == 1
    plane = lambda k: field[pl.ds(k * height, height), :]
    first, second = z_first[...], z_second[...]
    low, high = jnp.where(z_odd, first, second), jnp.where(z_odd, second, first)
    if late:
        low, high = (low + z_low[...]) * THIRD, (high + z_high[...]) * THIRD
    low = jnp.where(z_index == 0, plane(0), low)
    high = jnp.where(z_index == lax.axis_size("gz") - 1, plane(depth - 1), high)
    width = field.shape[1]
    rows = lax.broadcasted_iota(jnp.int32, (height, width), 0)
    lanes = lax.broadcasted_iota(jnp.int32, (height, width), 1)
    y_begin, y_end = y_index == 0, y_index == lax.axis_size("xy") - 1

    def g_rows(k):
        here = plane(k)
        slope = (plane(k + 1) if k < depth - 1 else high) - (plane(k - 1) if k else low)
        squares = (slope * 0.5) * (slope * 0.5)
        one, two = y_first[pl.ds(k, 1), :], y_second[pl.ds(k, 1), :]
        near, far = jnp.where(y_odd, one, two), jnp.where(y_odd, two, one)
        near = jnp.where(y_begin, here[:1], near)
        far = jnp.where(y_end, here[height - 1 :], far)
        after = jnp.where(rows == height - 1, far, pltpu.roll(here, height - 1, 0))
        before = jnp.where(rows == 0, near, pltpu.roll(here, 1, 0))
        slope = (after - before) * 0.5
        squares = squares + slope * slope
        after = jnp.where(lanes == width - 1, here, pltpu.roll(here, width - 1, 1))
        before = jnp.where(lanes == 0, here, pltpu.roll(here, 1, 1))
        slope = (after - before) * 0.5
        squares = squares + slope * slope
        g = 1.0 / (1.0 + squares * (1.0 / CONTRAST))
        g_out[pl.ds(k * height, height), :] = g
        return g

    chain(g_rows, plane, depth, solved, head, tail, element)


def y_kernel(depth, height, g_field, field, solved, head, tail, element):
    g_rows = lambda k: g_field[pl.ds(k, depth, stride=height), :]
    v_rows = lambda k: field[pl.ds(k, depth, stride=height), :]
    chain(g_rows, v_rows, height, solved, head, tail, element)


def x_kernel(first, rows, g_field, field, solved):
    width = field.shape[1]
    at = pl.ds(first, rows)
    g, right = g_field[at, :], field[at, :]
    lanes = lax.broadcasted_iota(jnp.int32, (rows, width), 1)
    link = jnp.where(lanes == width - 1, 0.0, HALF_LINK * (g + pltpu.roll(g, width - 1, 1)))
    main = 1.0 + link + pltpu.roll(link, 1, 1)
    stride = 1
    while stride < width:
        inverse = 1.0 / main
        factor = link * inverse
        back = width - stride
        ahead = link * pltpu.roll(inverse, back, 1)
        main = main - pltpu.roll(link * factor, stride, 1) - link * ahead
        right = right + pltpu.roll(factor * right, stride, 1) + ahead * pltpu.roll(right, back, 1)
        link = ahead * pltpu.roll(link, back, 1)
        stride *= 2
    solved[...] = right / main


def join(lower, upper_piece):
    link = HALF_LINK * (lower[6] + upper_piece[5])
    inverse = 1.0 / (1.0 + link * (lower[2] + upper_piece[0]))
    return link, inverse, lower[4] - upper_piece[3]


def sides(upper, own, got, last):
    pick = lambda a, b: jnp.where(upper, a, b)
    if not last:
        return [pick(got[k], own[k]) for k in range(7)], [pick(own[k], got[k]) for k in range(7)]
    zero = jnp.zeros_like(own[0])
    lower = [None, zero, pick(got[0], own[2]), None, pick(got[1], own[4]), None, pick(got[2], own[6])]
    return lower, [pick(own[0], got[0]), zero, None, pick(own[3], got[1]), None, pick(own[5], got[2]), None]


def is_upper(axis, level):
    return lax.rem(lax.div(lax.axis_index(axis), 1 << level), 2) == 1


def parts(ref, rows):
    if len(ref.shape) == 3:
        return [ref[k] for k in range(ref.shape[0])]
    return [ref[pl.ds(k * rows, rows), :] for k in range(3)]


def merge_kernel(axis, level, notes, own, got, *refs):
    outs = refs[notes:]
    upper = is_upper(axis, level)
    lower, higher = sides(upper, own, got, False)
    link, inverse, gap = join(lower, higher)
    share = link * inverse
    first, second = share * lower[1], share * higher[1]
    merged = [
        lower[0] - first * lower[1],
        first * higher[1],
        higher[2] - second * higher[1],
        lower[3] - first * gap,
        higher[4] + second * gap,
        lower[5],
        higher[6],
    ]
    for k in range(7):
        outs[0][k] = merged[k]
    if len(outs) > 1:
        above = is_upper(axis, level + 1)
        rows = own.shape[1]
        for k, (high, low) in enumerate(((0, 2), (3, 4), (5, 6))):
            outs[1][pl.ds(k * rows, rows), :] = jnp.where(above, merged[high], merged[low])
        if notes:
            outs[1][pl.ds(3 * rows, refs[0].shape[0]), :] = refs[0][...]


def unwind(axis, pairs):
    zero = jnp.zeros_like(pairs[0][0])
    from_low = from_high = jump_low = jump_high = zero
    for level in range(len(pairs) // 2 - 1, -1, -1):
        upper = is_upper(axis, level)
        own, got = pairs[2 * level], pairs[2 * level + 1]
        lower, higher = sides(upper, own, got, level == len(pairs) // 2 - 1)
        link, inverse, gap = join(lower, higher)
        jump = (gap + lower[1] * from_low - higher[1] * from_high) * inverse
        flow = link * jump
        from_low, jump_low = jnp.where(upper, flow, from_low), jnp.where(upper, jump, jump_low)
        from_high, jump_high = jnp.where(upper, from_high, -flow), jnp.where(upper, jump_high, jump)
    return from_low, from_high, jump_low, jump_high


def sum_kernel(depth, height, edges, near_x, far_x, solved, head, tail, *refs):
    pairs, outs = refs[: len(refs) - 1 - 2 * edges], refs[len(refs) - 1 - 2 * edges :]
    total = outs[0]
    low, high, _, _ = unwind("xy", [parts(ref, depth) for ref in pairs])
    half = depth // 2
    for k in range(height):
        along_y = solved[k] + low * head[k] + high * tail[k]
        at = pl.ds(k, half, stride=height)
        total[at, :] = near_x[at, :] + along_y[:half]
        total[pl.ds(half * height + k, half, stride=height), :] = far_x[at, :] + along_y[half:]
    if edges:
        z_odd = lax.rem(lax.axis_index("gz"), 2) == 1
        bottom, top = total[pl.ds(0, height), :], total[pl.ds((depth - 1) * height, height), :]
        outs[1][...] = jnp.where(z_odd, bottom, top)
        outs[2][...] = jnp.where(z_odd, top, bottom)


def step_kernel(depth, height, total, solved, head, tail, *refs):
    field, y_first, y_second, z_low, z_high = refs[-5:]
    low, high, jump_low, jump_high = unwind("gz", [parts(ref, height) for ref in refs[:-5]])
    for k in range(depth):
        at = pl.ds(k * height, height)
        along_z = solved[k] + low * head[k] + high * tail[k]
        if k == 0:
            z_low[...] = along_z + jump_low
        if k == depth - 1:
            z_high[...] = along_z - jump_high
        field[at, :] = (total[at, :] + along_z) * THIRD
    y_odd = lax.rem(lax.axis_index("xy"), 2) == 1
    near = field[pl.ds(0, depth, stride=height), :]
    far = field[pl.ds(height - 1, depth, stride=height), :]
    y_first[...] = jnp.where(y_odd, near, far)
    y_second[...] = jnp.where(y_odd, far, near)


def last_kernel(depth, height, total, solved, head, tail, *refs):
    field, halves = refs[-1 - CHUNKS], refs[-CHUNKS:]
    low, high, _, _ = unwind("gz", [parts(ref, height) for ref in refs[: -1 - CHUNKS]])
    planes, piece = BLOCK_ROWS // height, BLOCK_ROWS // CHUNKS
    for k in range(depth):
        at = pl.ds(k * height, height)
        value = (total[at, :] + (solved[k] + low * head[k] + high * tail[k])) * THIRD
        field[at, :] = value
        block, row = k // planes, (k % planes) * height
        halves[row // piece][block, pl.ds(row % piece, height), :] = value


def pack_kernel(ways, blocks, slots, *outs):
    place = lax.rem(lax.axis_index("gz"), ways)
    base = lax.axis_index("gz") - place
    for out in outs:
        out[...] = jnp.zeros_like(out)
    for block in range(blocks.shape[0]):
        slot = jnp.max(slots[pl.ds(block, 1), :]).astype(jnp.int32)
        rank, target = lax.rem(slot, MOST), lax.div(slot, MOST) - base
        for way, out in enumerate(outs):

            @pl.when(target == lax.bitwise_xor(place, way))
            def _():
                out[rank] = blocks[block]


def pack(ways, blocks, slots, name, after=()):
    shape = (MOST,) + blocks.shape[1:]
    return call(functools.partial(pack_kernel, ways), [shape] * ways, [blocks, slots], name, after=after)


def place_kernel(plan, count, *refs):
    incoming, sems = refs[-2:]
    me = lax.axis_index("gz")
    copies = []
    for k, (way, row) in enumerate(plan):
        rows = refs[k].shape[1]
        source = lax.bitwise_xor(me, way)
        target = incoming.at[pl.ds(source * MOST, MOST), pl.ds(row, rows), :]
        copies.append(pltpu.make_async_copy(refs[k], target, sems.at[k]))
    for copy in copies:
        copy.start()
    for copy in copies:
        copy.wait()


def place(arrays, plan, incoming, shape, name):
    count = len(arrays)
    extra = [] if incoming is None else [incoming]
    return pl.pallas_call(
        functools.partial(place_kernel, plan, count),
        out_shape=jax.ShapeDtypeStruct(shape, jnp.float32),
        in_specs=[pl.BlockSpec(memory_space=VMEM)] * count + [pl.BlockSpec(memory_space=pl.ANY)] * len(extra),
        out_specs=pl.BlockSpec(memory_space=pl.ANY),
        scratch_shapes=[pltpu.SemaphoreType.DMA((count,))],
        input_output_aliases={count: 0} if extra else {},
        compiler_params=pltpu.CompilerParams(vmem_limit_bytes=VMEM_LIMIT),
        name=name,
    )(*arrays, *extra)


def swap(values, axis, stride):
    count = lax.axis_size(axis)
    return lax.ppermute(values, axis, [(i, i ^ stride) for i in range(count)])


def neighbours(first, second, axis):
    count = lax.axis_size(axis)
    if axis == "xy":
        other = [(i, (i + 1) % count) for i in range(1, count, 2)]
        got = lax.ppermute(second, axis, other + [(j, i) for i, j in other])
    else:
        near = lax.axis_size("xy")
        pairs = []
        for i in range(count):
            end = i in (0, count - 1)
            j = i if end else i + 1 if i % 2 else i - 1
            pairs += [(i * near + c, j * near + (c ^ 1 if end else c)) for c in range(near)]
        got = lax.ppermute(second, (axis, "xy"), pairs)
    return swap(first, axis, 1), got


def merge(element, got, axis, level, after=(), notes=()):
    rows, width = element.shape[1:]
    last = 4 << level >= lax.axis_size(axis)
    notes = notes if last else ()
    outs = [element.shape] + [(3 * rows + sum(note.shape[0] for note in notes), width)] * last
    merged = call(
        functools.partial(merge_kernel, axis, level, len(notes)),
        outs,
        [element, got, *notes],
        f"merge_{axis}_{level}",
        after=after,
    )
    return merged[0], merged[-1]


def route(halves, blocks, slots, across):
    count, width = lax.axis_size("gz"), blocks.shape[2]
    ways, piece = count // 2, BLOCK_ROWS // CHUNKS
    crossed = [swap(half, "gz", ways) for half in halves]
    straight = pack(ways, blocks, slots, "straight")
    arrays = [straight[0]] + [swap(straight[way], "gz", way) for way in range(1, ways)]
    shape = (count * MOST, BLOCK_ROWS, width)
    incoming = place(arrays, [(way, 0) for way in range(ways)], None, shape, "place_straight")
    for chunk in range(CHUNKS):
        passed = pack(ways, crossed[chunk], across, f"relay_{chunk}")
        arrays = [passed[0]] + [swap(passed[way], "gz", way) for way in range(1, ways)]
        plan = [(way ^ ways, chunk * piece) for way in range(ways)]
        incoming = place(arrays, plan, incoming, shape, f"place_{chunk}")
    return incoming


def on_device(volume, owners):
    depth, height, width = volume.shape
    z_count, y_count = lax.axis_size("gz"), lax.axis_size("xy")
    z_rounds, y_rounds = z_count.bit_length() - 1, y_count.bit_length() - 1
    blocks = owners.shape[1]
    flat, plane, side = (depth * height, width), (height, width), (depth, width)
    z_parts, y_parts = (depth, height, width), (height, depth, width)
    part = functools.partial
    field = volume.reshape(flat)
    edges = call(part(edge_kernel, depth, height), [plane, plane, side, side], [field], "edges")
    z_sides, y_sides = neighbours(*edges[:2], "gz"), neighbours(*edges[2:], "xy")
    (slots,) = call(
        slot_kernel, [(-(-blocks // 8) * 8, width)], [owners.reshape(1, blocks)], "slots", smem=(0,), after=edges[:1]
    )
    ghosts = ()
    for step in range(STEPS):
        last = step == STEPS - 1
        g_field, *z_pieces, z_element = call(
            part(z_kernel, depth, height, step > 0),
            [flat, z_parts, z_parts, z_parts, (7,) + plane],
            [field, *z_sides, *y_sides, *ghosts],
            "z_pieces",
        )
        *y_pieces, y_element = call(
            part(y_kernel, depth, height),
            [y_parts, y_parts, y_parts, (7,) + side],
            [g_field, field],
            "y_pieces",
            after=[z_element],
        )
        y_sent, y_pairs = y_element, []
        z_sent, z_pairs = z_element, []
        for level in range(y_rounds):
            y_pairs += [y_element, swap(y_sent, "xy", 1 << level)]
            if level + 1 < y_rounds:
                y_element, y_sent = merge(*y_pairs[-2:], "xy", level)
        half = (depth // 2 * height, width)
        for level in range(z_rounds):
            z_pairs += [z_element, swap(z_sent, "gz", 1 << level)]
            behind = []
            if level == 0:
                (near_x,) = call(
                    part(x_kernel, 0, half[0]), [half], [g_field, field], "x_near", after=[y_element]
                )
                behind = [near_x]
            if level == 1:
                (far_x,) = call(
                    part(x_kernel, half[0], half[0]), [half], [g_field, field], "x_far", after=[z_element]
                )
                total, *z_edges = call(
                    part(sum_kernel, depth, height, not last),
                    [flat] + [plane, plane] * (not last),
                    [near_x, far_x, *y_pieces, *y_pairs],
                    "sum_xy",
                )
                behind = [total]
            if level + 1 < z_rounds:
                z_element, z_sent = merge(*z_pairs[-2:], "gz", level, behind, () if step else (slots,))
        if step == 0:
            across = z_pairs[-1][3 * height :]
        if not last:
            z_sides = neighbours(*z_edges, "gz")
            field, *rest = call(
                part(step_kernel, depth, height),
                [flat, side, side, plane, plane],
                [total, *z_pieces, *z_pairs],
                "new_field",
            )
            y_sides, ghosts = neighbours(*rest[:2], "xy"), rest[2:]
    field, *halves = call(
        part(last_kernel, depth, height),
        [flat] + [(blocks, BLOCK_ROWS // CHUNKS, width)] * CHUNKS,
        [total, *z_pieces, *z_pairs],
        "denoised",
    )
    incoming = route(halves, field.reshape(blocks, BLOCK_ROWS, width), slots, across)
    return field.reshape(volume.shape), incoming[None]


def solution(mesh):
    in_specs = (P("gz", "xy", None), P("xy", "gz", None))
    out_specs = (P("gz", "xy", None), P("xy", "gz", None, None))
    return jax.shard_map(
        on_device, mesh=mesh, in_specs=in_specs, out_specs=out_specs, check_vma=False
    )
```

```python
import functools

import jax
import jax.numpy as jnp
from jax import lax
from jax.experimental import pallas as pl
from jax.experimental.pallas import tpu as pltpu
from jax.sharding import PartitionSpec as P


STEPS = 2
MOST = 2
CHUNKS = 2
BLOCK_ROWS = 128
TIME_STEP = 30.0
CONTRAST = 4.0
HALF_LINK = 1.5 * TIME_STEP
THIRD = 1.0 / 3.0
VMEM_LIMIT = 16 * 1024 * 1024
VMEM = pltpu.VMEM


def call(body, outs, ins, smem=(), after=()):
    count = len(ins)
    specs = [
        pl.BlockSpec(memory_space=pltpu.SMEM if k in smem else VMEM) for k in range(count)
    ] + [pl.BlockSpec(memory_space=pl.ANY)] * len(after)
    return pl.pallas_call(
        lambda *refs: body(*refs[:count], *refs[count + len(after) :]),
        out_shape=[jax.ShapeDtypeStruct(shape, jnp.float32) for shape in outs],
        in_specs=specs,
        out_specs=[pl.BlockSpec(memory_space=VMEM)] * len(outs),
        compiler_params=pltpu.CompilerParams(vmem_limit_bytes=VMEM_LIMIT),
    )(*ins, *after)


def edge_kernel(depth, height, field, z_first, z_second, y_first, y_second):
    z_odd = lax.rem(lax.axis_index("gz"), 2) == 1
    y_odd = lax.rem(lax.axis_index("xy"), 2) == 1
    bottom, top = field[pl.ds(0, height), :], field[pl.ds((depth - 1) * height, height), :]
    z_first[...] = jnp.where(z_odd, bottom, top)
    z_second[...] = jnp.where(z_odd, top, bottom)
    near = field[pl.ds(0, depth, stride=height), :]
    far = field[pl.ds(height - 1, depth, stride=height), :]
    y_first[...] = jnp.where(y_odd, near, far)
    y_second[...] = jnp.where(y_odd, far, near)


def slot_kernel(owners, slots):
    slots[...] = jnp.zeros_like(slots)
    for block in range(owners.shape[1]):
        rank = jnp.int32(0)
        for other in range(block):
            rank = rank + (owners[0, other] == owners[0, block]).astype(jnp.int32)
        slot = owners[0, block] * MOST + rank
        slots[pl.ds(block, 1), :] = jnp.full((1, slots.shape[1]), slot.astype(jnp.float32))


def chain(g_rows, v_rows, count, solved, head, tail, element):
    g_head = g_prev = g_rows(0)
    pivot = jnp.ones_like(g_prev)
    right = v_rows(0)
    unit = pivot
    for k in range(count - 1):
        g_next = g_rows(k + 1)
        link = HALF_LINK * (g_prev + g_next)
        inverse = 1.0 / (pivot + link)
        ratio = link * inverse
        solved[k] = right * inverse
        head[k] = unit * inverse
        tail[k] = ratio
        pivot = 1.0 + ratio * pivot
        right = v_rows(k + 1) + ratio * right
        unit = ratio * unit
        g_prev = g_next
    inverse = 1.0 / pivot
    value, from_head, from_tail = right * inverse, unit * inverse, inverse
    solved[count - 1] = value
    head[count - 1] = from_head
    tail[count - 1] = from_tail
    element[2] = from_tail
    element[4] = value
    element[5] = g_head
    element[6] = g_prev
    for k in range(count - 2, -1, -1):
        ratio = tail[k]
        value = solved[k] + ratio * value
        from_head = head[k] + ratio * from_head
        from_tail = ratio * from_tail
        solved[k] = value
        head[k] = from_head
        tail[k] = from_tail
    element[0] = from_head
    element[1] = from_tail
    element[3] = value


def z_kernel(depth, height, late, *refs):
    if late:
        field, z_first, z_second, y_first, y_second, z_low, z_high = refs[:7]
    else:
        field, z_first, z_second, y_first, y_second = refs[:5]
    g_out, solved, head, tail, element = refs[-5:]
    z_index, y_index = lax.axis_index("gz"), lax.axis_index("xy")
    z_odd, y_odd = lax.rem(z_index, 2) == 1, lax.rem(y_index, 2) == 1
    plane = lambda k: field[pl.ds(k * height, height), :]
    first, second = z_first[...], z_second[...]
    low, high = jnp.where(z_odd, first, second), jnp.where(z_odd, second, first)
    if late:
        low, high = (low + z_low[...]) * THIRD, (high + z_high[...]) * THIRD
    low = jnp.where(z_index == 0, plane(0), low)
    high = jnp.where(z_index == lax.axis_size("gz") - 1, plane(depth - 1), high)
    width = field.shape[1]
    rows = lax.broadcasted_iota(jnp.int32, (height, width), 0)
    lanes = lax.broadcasted_iota(jnp.int32, (height, width), 1)
    y_begin, y_end = y_index == 0, y_index == lax.axis_size("xy") - 1

    def g_rows(k):
        here = plane(k)
        slope = (plane(k + 1) if k < depth - 1 else high) - (plane(k - 1) if k else low)
        squares = (slope * 0.5) * (slope * 0.5)
        one, two = y_first[pl.ds(k, 1), :], y_second[pl.ds(k, 1), :]
        near, far = jnp.where(y_odd, one, two), jnp.where(y_odd, two, one)
        near = jnp.where(y_begin, here[:1], near)
        far = jnp.where(y_end, here[height - 1 :], far)
        after = jnp.where(rows == height - 1, far, pltpu.roll(here, height - 1, 0))
        before = jnp.where(rows == 0, near, pltpu.roll(here, 1, 0))
        slope = (after - before) * 0.5
        squares = squares + slope * slope
        after = jnp.where(lanes == width - 1, here, pltpu.roll(here, width - 1, 1))
        before = jnp.where(lanes == 0, here, pltpu.roll(here, 1, 1))
        slope = (after - before) * 0.5
        squares = squares + slope * slope
        g = 1.0 / (1.0 + squares * (1.0 / CONTRAST))
        g_out[pl.ds(k * height, height), :] = g
        return g

    chain(g_rows, plane, depth, solved, head, tail, element)


def y_kernel(depth, height, g_field, field, solved, head, tail, element):
    g_rows = lambda k: g_field[pl.ds(k, depth, stride=height), :]
    v_rows = lambda k: field[pl.ds(k, depth, stride=height), :]
    chain(g_rows, v_rows, height, solved, head, tail, element)


def x_kernel(first, rows, g_field, field, solved):
    width = field.shape[1]
    at = pl.ds(first, rows)
    g, right = g_field[at, :], field[at, :]
    lanes = lax.broadcasted_iota(jnp.int32, (rows, width), 1)
    link = jnp.where(lanes == width - 1, 0.0, HALF_LINK * (g + pltpu.roll(g, width - 1, 1)))
    main = 1.0 + link + pltpu.roll(link, 1, 1)
    stride = 1
    while stride < width:
        inverse = 1.0 / main
        factor = link * inverse
        back = width - stride
        ahead = link * pltpu.roll(inverse, back, 1)
        main = main - pltpu.roll(link * factor, stride, 1) - link * ahead
        right = right + pltpu.roll(factor * right, stride, 1) + ahead * pltpu.roll(right, back, 1)
        link = ahead * pltpu.roll(link, back, 1)
        stride *= 2
    solved[...] = right / main


def join(lower, upper_piece):
    link = HALF_LINK * (lower[6] + upper_piece[5])
    inverse = 1.0 / (1.0 + link * (lower[2] + upper_piece[0]))
    return link, inverse, lower[4] - upper_piece[3]


def sides(upper, own, got, last):
    pick = lambda a, b: jnp.where(upper, a, b)
    if not last:
        return [pick(got[k], own[k]) for k in range(7)], [pick(own[k], got[k]) for k in range(7)]
    zero = jnp.zeros_like(own[0])
    lower = [None, zero, pick(got[0], own[2]), None, pick(got[1], own[4]), None, pick(got[2], own[6])]
    return lower, [pick(own[0], got[0]), zero, None, pick(own[3], got[1]), None, pick(own[5], got[2]), None]


def is_upper(axis, level):
    return lax.rem(lax.div(lax.axis_index(axis), 1 << level), 2) == 1


def parts(ref, rows):
    if len(ref.shape) == 3:
        return [ref[k] for k in range(ref.shape[0])]
    return [ref[pl.ds(k * rows, rows), :] for k in range(3)]


def merge_kernel(axis, level, notes, own, got, *refs):
    outs = refs[notes:]
    upper = is_upper(axis, level)
    lower, higher = sides(upper, own, got, False)
    link, inverse, gap = join(lower, higher)
    share = link * inverse
    first, second = share * lower[1], share * higher[1]
    merged = [
        lower[0] - first * lower[1],
        first * higher[1],
        higher[2] - second * higher[1],
        lower[3] - first * gap,
        higher[4] + second * gap,
        lower[5],
        higher[6],
    ]
    for k in range(7):
        outs[0][k] = merged[k]
    if len(outs) > 1:
        above = is_upper(axis, level + 1)
        rows = own.shape[1]
        for k, (high, low) in enumerate(((0, 2), (3, 4), (5, 6))):
            outs[1][pl.ds(k * rows, rows), :] = jnp.where(above, merged[high], merged[low])
        if notes:
            outs[1][pl.ds(3 * rows, refs[0].shape[0]), :] = refs[0][...]


def unwind(axis, pairs):
    zero = jnp.zeros_like(pairs[0][0])
    from_low = from_high = jump_low = jump_high = zero
    for level in range(len(pairs) // 2 - 1, -1, -1):
        upper = is_upper(axis, level)
        own, got = pairs[2 * level], pairs[2 * level + 1]
        lower, higher = sides(upper, own, got, level == len(pairs) // 2 - 1)
        link, inverse, gap = join(lower, higher)
        jump = (gap + lower[1] * from_low - higher[1] * from_high) * inverse
        flow = link * jump
        from_low, jump_low = jnp.where(upper, flow, from_low), jnp.where(upper, jump, jump_low)
        from_high, jump_high = jnp.where(upper, from_high, -flow), jnp.where(upper, jump_high, jump)
    return from_low, from_high, jump_low, jump_high


def sum_kernel(depth, height, edges, near_x, far_x, solved, head, tail, *refs):
    pairs, outs = refs[: len(refs) - 1 - 2 * edges], refs[len(refs) - 1 - 2 * edges :]
    total = outs[0]
    low, high, _, _ = unwind("xy", [parts(ref, depth) for ref in pairs])
    half = depth // 2
    for k in range(height):
        along_y = solved[k] + low * head[k] + high * tail[k]
        at = pl.ds(k, half, stride=height)
        total[at, :] = near_x[at, :] + along_y[:half]
        total[pl.ds(half * height + k, half, stride=height), :] = far_x[at, :] + along_y[half:]
    if edges:
        z_odd = lax.rem(lax.axis_index("gz"), 2) == 1
        bottom, top = total[pl.ds(0, height), :], total[pl.ds((depth - 1) * height, height), :]
        outs[1][...] = jnp.where(z_odd, bottom, top)
        outs[2][...] = jnp.where(z_odd, top, bottom)


def step_kernel(depth, height, total, solved, head, tail, *refs):
    field, y_first, y_second, z_low, z_high = refs[-5:]
    low, high, jump_low, jump_high = unwind("gz", [parts(ref, height) for ref in refs[:-5]])
    for k in range(depth):
        at = pl.ds(k * height, height)
        along_z = solved[k] + low * head[k] + high * tail[k]
        if k == 0:
            z_low[...] = along_z + jump_low
        if k == depth - 1:
            z_high[...] = along_z - jump_high
        field[at, :] = (total[at, :] + along_z) * THIRD
    y_odd = lax.rem(lax.axis_index("xy"), 2) == 1
    near = field[pl.ds(0, depth, stride=height), :]
    far = field[pl.ds(height - 1, depth, stride=height), :]
    y_first[...] = jnp.where(y_odd, near, far)
    y_second[...] = jnp.where(y_odd, far, near)


def last_kernel(depth, height, total, solved, head, tail, *refs):
    chunks = refs[-CHUNKS:]
    low, high, _, _ = unwind("gz", [parts(ref, height) for ref in refs[:-CHUNKS]])
    planes, piece = BLOCK_ROWS // height, BLOCK_ROWS // CHUNKS
    for k in range(depth):
        value = (total[pl.ds(k * height, height), :] + (solved[k] + low * head[k] + high * tail[k])) * THIRD
        block, row = k // planes, (k % planes) * height
        chunks[row // piece][block, pl.ds(row % piece, height), :] = value


def pack_kernel(ways, count, *refs):
    pieces, slots, outs = refs[:count], refs[count], refs[count + 1 :]
    me = lax.axis_index("gz")
    place = lax.rem(me, ways)
    number, rows = pieces[0].shape[:2]
    placed = [jnp.max(slots[pl.ds(block, 1), :]).astype(jnp.int32) for block in range(number)]
    for out in outs:
        out[...] = jnp.zeros_like(out)
    for block, slot in enumerate(placed):
        rank, target = lax.rem(slot, MOST), lax.div(slot, MOST) - (me - place)
        for way, out in enumerate(outs):

            @pl.when(target == lax.bitwise_xor(place, way))
            def _():
                for k, piece in enumerate(pieces):
                    out[rank, pl.ds(k * rows, rows), :] = piece[block]


def pack(ways, pieces, slots):
    rows, width = pieces[0].shape[1:]
    shape = (MOST, rows * len(pieces), width)
    return call(functools.partial(pack_kernel, ways, len(pieces)), [shape] * ways, [*pieces, slots])


def place_kernel(plan, kept, fresh, *refs):
    count = len(plan) + kept
    outs, sems = refs[count + (not fresh) : -1], refs[-1]
    me = lax.axis_index("gz")
    copies = []
    for k in range(count):
        rows = refs[k].shape[1]
        if k < len(plan):
            way, row = plan[k]
            source = lax.bitwise_xor(me, way)
            target = outs[0].at[pl.ds(source * MOST, MOST), pl.ds(row, rows), :]
        else:
            target = outs[1].at[:, pl.ds((k - len(plan)) * rows, rows), :]
        copies.append(pltpu.make_async_copy(refs[k], target, sems.at[k]))
    for copy in copies:
        copy.start()
    for copy in copies:
        copy.wait()


def place(arrays, plan, incoming, shapes, kept=()):
    count = len(arrays) + len(kept)
    extra = [] if incoming is None else [incoming]
    return pl.pallas_call(
        functools.partial(place_kernel, plan, len(kept), not extra),
        out_shape=[jax.ShapeDtypeStruct(shape, jnp.float32) for shape in shapes],
        in_specs=[pl.BlockSpec(memory_space=VMEM)] * count + [pl.BlockSpec(memory_space=pl.ANY)] * len(extra),
        out_specs=[pl.BlockSpec(memory_space=pl.ANY)] * len(shapes),
        scratch_shapes=[pltpu.SemaphoreType.DMA((count,))],
        input_output_aliases={count: 0} if extra else {},
        compiler_params=pltpu.CompilerParams(vmem_limit_bytes=VMEM_LIMIT),
    )(*arrays, *kept, *extra)


def swap(values, axis, stride):
    count = lax.axis_size(axis)
    return lax.ppermute(values, axis, [(i, i ^ stride) for i in range(count)])


def near(first, axis):
    return swap(first, axis, 1)


def far(second, axis):
    count = lax.axis_size(axis)
    if axis == "xy":
        other = [(i, (i + 1) % count) for i in range(1, count, 2)]
        return lax.ppermute(second, axis, other + [(j, i) for i, j in other])
    beside = lax.axis_size("xy")
    pairs = []
    for i in range(count):
        end = i in (0, count - 1)
        j = i if end else i + 1 if i % 2 else i - 1
        pairs += [(i * beside + c, j * beside + (c ^ 1 if end else c)) for c in range(beside)]
    return lax.ppermute(second, (axis, "xy"), pairs)


def neighbours(first, second, axis):
    got = far(second, axis)
    return near(first, axis), got


def merge(element, got, axis, level, after=(), notes=()):
    rows, width = element.shape[1:]
    last = 4 << level >= lax.axis_size(axis)
    notes = notes if last else ()
    outs = [element.shape] + [(3 * rows + sum(note.shape[0] for note in notes), width)] * last
    merged = call(functools.partial(merge_kernel, axis, level, len(notes)), outs, [element, got, *notes], after=after)
    return merged[0], merged[-1]


def route(chunks, slots, across):
    count = lax.axis_size("gz")
    number, piece, width = chunks[0].shape
    ways = count // 2
    crossed = [swap(chunk, "gz", ways) for chunk in chunks]
    straight = pack(ways, chunks, slots)
    arrays = [straight[0]] + [swap(straight[way], "gz", way) for way in range(1, ways)]
    shapes = [(count * MOST, BLOCK_ROWS, width), (number, BLOCK_ROWS, width)]
    plan = [(way, 0) for way in range(ways)]
    incoming, field = place(arrays, plan, None, shapes, chunks)
    for k in range(CHUNKS):
        passed = pack(ways, crossed[k : k + 1], across)
        arrays = [passed[0]] + [swap(passed[way], "gz", way) for way in range(1, ways)]
        plan = [(way ^ ways, k * piece) for way in range(ways)]
        (incoming,) = place(arrays, plan, incoming, shapes[:1])
    return field, incoming


def on_device(volume, owners):
    depth, height, width = volume.shape
    z_count, y_count = lax.axis_size("gz"), lax.axis_size("xy")
    z_rounds, y_rounds = z_count.bit_length() - 1, y_count.bit_length() - 1
    blocks = owners.shape[1]
    flat, plane, side = (depth * height, width), (height, width), (depth, width)
    z_parts, y_parts = (depth, height, width), (height, depth, width)
    part = functools.partial
    field = volume.reshape(flat)
    edges = call(part(edge_kernel, depth, height), [plane, plane, side, side], [field])
    z_sides, y_sides = neighbours(*edges[:2], "gz"), neighbours(*edges[2:], "xy")
    (slots,) = call(
        slot_kernel, [(-(-blocks // 8) * 8, width)], [owners.reshape(1, blocks)], smem=(0,), after=edges[:1]
    )
    ghosts = ()
    for step in range(STEPS):
        last = step == STEPS - 1
        g_field, *z_pieces, z_element = call(
            part(z_kernel, depth, height, step > 0),
            [flat, z_parts, z_parts, z_parts, (7,) + plane],
            [field, *z_sides, *y_sides, *ghosts],
            after=[slots],
        )
        *y_pieces, y_element = call(
            part(y_kernel, depth, height), [y_parts, y_parts, y_parts, (7,) + side], [g_field, field], after=[z_element]
        )
        y_sent, y_pairs = y_element, []
        z_sent, z_pairs = z_element, []
        for level in range(y_rounds):
            y_pairs += [y_element, swap(y_sent, "xy", 1 << level)]
            if level + 1 < y_rounds:
                y_element, y_sent = merge(*y_pairs[-2:], "xy", level)
        half = (depth // 2 * height, width)
        for level in range(z_rounds):
            z_pairs += [z_element, swap(z_sent, "gz", 1 << level)]
            behind = []
            if level == 0:
                (near_x,) = call(part(x_kernel, 0, half[0]), [half], [g_field, field], after=[y_element])
                behind = [near_x]
            if level == 1:
                (far_x,) = call(part(x_kernel, half[0], half[0]), [half], [g_field, field], after=[z_element])
                total, *z_edges = call(
                    part(sum_kernel, depth, height, not last),
                    [flat] + [plane, plane] * (not last),
                    [near_x, far_x, *y_pieces, *y_pairs],
                )
                behind = [far_x]
            if level + 1 < z_rounds:
                z_element, z_sent = merge(*z_pairs[-2:], "gz", level, behind, () if step else (slots,))
        if step == 0:
            across = z_pairs[-1][3 * height :]
        if not last:
            z_sides = neighbours(*z_edges, "gz")
            field, *rest = call(
                part(step_kernel, depth, height), [flat, side, side, plane, plane], [total, *z_pieces, *z_pairs]
            )
            y_sides, ghosts = neighbours(*rest[:2], "xy"), rest[2:]
    chunks = call(
        part(last_kernel, depth, height), [(blocks, BLOCK_ROWS // CHUNKS, width)] * CHUNKS, [total, *z_pieces, *z_pairs]
    )
    field, incoming = route(chunks, slots, across)
    return field.reshape(volume.shape), incoming[None]


def solution(mesh):
    in_specs = (P("gz", "xy", None), P("xy", "gz", None))
    out_specs = (P("gz", "xy", None), P("xy", "gz", None, None))

    return jax.shard_map(on_device, mesh=mesh, in_specs=in_specs, out_specs=out_specs, check_vma=False)
```

```python
import functools

import jax
import jax.numpy as jnp
from jax import lax
from jax.experimental import pallas as pl
from jax.experimental.pallas import tpu as pltpu
from jax.sharding import PartitionSpec as P


MOST = 2
CHUNKS = (128,)
BLOCK_ROWS = 128
TIME_STEP = 30.0
CONTRAST = 4.0
HALF_LINK = 1.5 * TIME_STEP
THIRD = 1.0 / 3.0
GHOSTS = 8
LAST_SENT = ((0, 2), (3, 4), (5, 6))
VMEM_LIMIT = 16 * 1024 * 1024
VMEM = pltpu.VMEM


def call(body, outs, ins, after=()):
    count = len(ins)
    specs = [pl.BlockSpec(memory_space=VMEM)] * count + [pl.BlockSpec(memory_space=pl.ANY)] * len(after)
    return pl.pallas_call(
        lambda *refs: body(*refs[:count], *refs[count + len(after) :]),
        out_shape=[jax.ShapeDtypeStruct(shape, jnp.float32) for shape in outs],
        in_specs=specs,
        out_specs=[pl.BlockSpec(memory_space=VMEM)] * len(outs),
        compiler_params=pltpu.CompilerParams(vmem_limit_bytes=VMEM_LIMIT),
    )(*ins, *after)


def edge_kernel(depth, height, field, y_first, y_second):
    y_odd = lax.rem(lax.axis_index("xy"), 2) == 1
    for k in range(2):
        near = field[pl.ds(k, depth, stride=height), :]
        far = field[pl.ds(height - 1 - k, depth, stride=height), :]
        y_first[pl.ds(k * depth, depth), :] = jnp.where(y_odd, near, far)
        y_second[pl.ds(k * depth, depth), :] = jnp.where(y_odd, far, near)


def slab_kernel(depth, height, field, y_first, y_second, slabs, z_first, z_second):
    slab = height + GHOSTS
    y_odd = lax.rem(lax.axis_index("xy"), 2) == 1
    for k in range(depth):
        slabs[pl.ds(k * slab, height), :] = field[pl.ds(k * height, height), :]
    for k in range(2):
        one, two = y_first[pl.ds(k * depth, depth), :], y_second[pl.ds(k * depth, depth), :]
        slabs[pl.ds(height + 2 * k, depth, stride=slab), :] = jnp.where(y_odd, one, two)
        slabs[pl.ds(height + 2 * k + 1, depth, stride=slab), :] = jnp.where(y_odd, two, one)
    for k in range(4, GHOSTS):
        slabs[pl.ds(height + k, depth, stride=slab), :] = jnp.zeros((depth, field.shape[1]), field.dtype)
    z_odd = lax.rem(lax.axis_index("gz"), 2) == 1
    for k in range(2):
        low, high = slabs[pl.ds(k * slab, slab), :], slabs[pl.ds((depth - 1 - k) * slab, slab), :]
        z_first[pl.ds(k * slab, slab), :] = jnp.where(z_odd, low, high)
        z_second[pl.ds(k * slab, slab), :] = jnp.where(z_odd, high, low)


def slot_kernel(given, first, slots, owners, sem):
    copy = pltpu.make_async_copy(given, owners, sem)
    copy.start()
    slots[...] = jnp.zeros_like(slots)
    copy.wait()
    for block in range(owners.shape[1]):
        rank = jnp.int32(0)
        for other in range(block):
            rank = rank + (owners[0, other] == owners[0, block]).astype(jnp.int32)
        slot = owners[0, block] * MOST + rank
        slots[pl.ds(block, 1), :] = jnp.full((1, slots.shape[1]), slot.astype(jnp.float32))


def slots_of(owners, width, after):
    blocks = owners.shape[1]
    return pl.pallas_call(
        slot_kernel,
        out_shape=jax.ShapeDtypeStruct((-(-blocks // 8) * 8, width), jnp.float32),
        in_specs=[pl.BlockSpec(memory_space=pl.ANY)] * 2,
        out_specs=pl.BlockSpec(memory_space=VMEM),
        scratch_shapes=[pltpu.SMEM((1, blocks), jnp.int32), pltpu.SemaphoreType.DMA],
        compiler_params=pltpu.CompilerParams(vmem_limit_bytes=VMEM_LIMIT),
        name="slots",
    )(owners.reshape(1, blocks), after)


def chain(g_rows, v_rows, count, solved, head, tail, element):
    g_head = g_prev = g_rows(0)
    pivot = jnp.ones_like(g_prev)
    right = v_rows(0)
    unit = pivot
    for k in range(count - 1):
        g_next = g_rows(k + 1)
        link = HALF_LINK * (g_prev + g_next)
        inverse = 1.0 / (pivot + link)
        ratio = link * inverse
        solved[k] = right * inverse
        head[k] = unit * inverse
        tail[k] = ratio
        pivot = 1.0 + ratio * pivot
        right = v_rows(k + 1) + ratio * right
        unit = ratio * unit
        g_prev = g_next
    inverse = 1.0 / pivot
    value, from_head, from_tail = right * inverse, unit * inverse, inverse
    solved[count - 1] = value
    head[count - 1] = from_head
    tail[count - 1] = from_tail
    element[2] = from_tail
    element[4] = value
    if element.shape[0] > 5:
        element[5] = g_head
        element[6] = g_prev
    for k in range(count - 2, -1, -1):
        ratio = tail[k]
        value = solved[k] + ratio * value
        from_head = head[k] + ratio * from_head
        from_tail = ratio * from_tail
        solved[k] = value
        head[k] = from_head
        tail[k] = from_tail
    element[0] = from_head
    element[1] = from_tail
    element[3] = value


def diffusivity(up, down, after, before, right, left):
    squares = ((up - down) * 0.5) * ((up - down) * 0.5)
    slope = (after - before) * 0.5
    squares = squares + slope * slope
    slope = (right - left) * 0.5
    squares = squares + slope * slope
    return 1.0 / (1.0 + squares * (1.0 / CONTRAST))


def x_sides(here):
    width = here.shape[1]
    lanes = lax.broadcasted_iota(jnp.int32, here.shape, 1)
    right = jnp.where(lanes == width - 1, here, pltpu.roll(here, width - 1, 1))
    return right, jnp.where(lanes == 0, here, pltpu.roll(here, 1, 1))


def ends(axis):
    index = lax.axis_index(axis)
    return index == 0, index == lax.axis_size(axis) - 1


def wide_kernel(depth, height, slabs, z_first, z_second, field, g_out, solved, head, tail, element, w_low, w_high):
    slab = height + GHOSTS
    width = slabs.shape[1]
    z_odd = lax.rem(lax.axis_index("gz"), 2) == 1
    z_begin, z_end = ends("gz")
    y_begin, y_end = ends("xy")
    rows = lax.broadcasted_iota(jnp.int32, (slab, width), 0)
    own = depth * slab
    field[pl.ds(0, own), :] = slabs[...]
    for k in range(2):
        one, two = z_first[pl.ds(k * slab, slab), :], z_second[pl.ds(k * slab, slab), :]
        field[pl.ds(own + 2 * k * slab, slab), :] = jnp.where(z_odd, one, two)
        field[pl.ds(own + (2 * k + 1) * slab, slab), :] = jnp.where(z_odd, two, one)
    spare = field.shape[0] - own - 4 * slab
    field[pl.ds(own + 4 * slab, spare), :] = jnp.zeros((spare, width), field.dtype)
    g_out[pl.ds(own + 2 * slab, spare + 2 * slab), :] = jnp.ones((spare + 2 * slab, width), field.dtype)

    def begin(k):
        if k < 0:
            return own + (2 if k < -1 else 0) * slab
        return own + (1 + 2 * (k - depth)) * slab if k >= depth else k * slab

    plane = lambda k: field[pl.ds(begin(k), slab), :]

    def g_rows(k):
        here, up, down = plane(k), plane(k + 1), plane(k - 1)
        if k == 0:
            down = jnp.where(z_begin, here, down)
        if k == depth - 1:
            up = jnp.where(z_end, here, up)
        row = lambda r: field[pl.ds(begin(k) + r, 1), :]
        first, final = row(0), row(height - 1)
        after = jnp.where(rows == height - 1, jnp.where(y_end, final, row(height + 1)), pltpu.roll(here, slab - 1, 0))
        after = jnp.where(rows == height, first, jnp.where(rows == height + 1, row(height + 3), after))
        before = jnp.where(rows == 0, jnp.where(y_begin, first, row(height)), pltpu.roll(here, 1, 0))
        before = jnp.where(rows == height, row(height + 2), jnp.where(rows == height + 1, final, before))
        g = diffusivity(up, down, after, before, *x_sides(here))
        g_out[pl.ds(begin(k), slab), :] = g
        return g

    chain(g_rows, plane, depth, solved, head, tail, element)
    g_own = lambda k: g_out[pl.ds(k * slab, slab), :]
    w_low[...] = HALF_LINK * (g_own(0) + g_rows(-1))
    link = HALF_LINK * (g_own(depth - 1) + g_rows(depth))
    w_high[...] = link
    element[2] = element[2] + 1.0 / link


def z_kernel(depth, height, field, near, far, low, high, g_out, solved, head, tail, element):
    plane = lambda k: field[pl.ds(k * height, height), :]
    z_begin, z_end = ends("gz")
    y_begin, y_end = ends("xy")
    below = jnp.where(z_begin, plane(0), low[...])
    above = jnp.where(z_end, plane(depth - 1), high[...])
    rows = lax.broadcasted_iota(jnp.int32, (height, field.shape[1]), 0)

    def g_rows(k):
        here = plane(k)
        up, down = plane(k + 1) if k < depth - 1 else above, plane(k - 1) if k else below
        first = jnp.where(y_begin, here[:1], near[pl.ds(k, 1), :])
        final = jnp.where(y_end, here[height - 1 :], far[pl.ds(k, 1), :])
        after = jnp.where(rows == height - 1, final, pltpu.roll(here, height - 1, 0))
        before = jnp.where(rows == 0, first, pltpu.roll(here, 1, 0))
        g = diffusivity(up, down, after, before, *x_sides(here))
        g_out[pl.ds(k * height, height), :] = g
        return g

    chain(g_rows, plane, depth, solved, head, tail, element)


def y_kernel(planes, height, slab, g_field, field, solved, head, tail, element):
    g_rows = lambda k: g_field[pl.ds(k, planes, stride=slab), :]
    v_rows = lambda k: field[pl.ds(k, planes, stride=slab), :]
    chain(g_rows, v_rows, height, solved, head, tail, element)


def x_kernel(first, rows, g_field, field, solved):
    width = field.shape[1]
    at = pl.ds(first, rows)
    g, right = g_field[at, :], field[at, :]
    lanes = lax.broadcasted_iota(jnp.int32, (rows, width), 1)
    link = jnp.where(lanes == width - 1, 0.0, HALF_LINK * (g + pltpu.roll(g, width - 1, 1)))
    main = 1.0 + link + pltpu.roll(link, 1, 1)
    stride = 1
    while stride < width:
        inverse = 1.0 / main
        factor = link * inverse
        back = width - stride
        ahead = link * pltpu.roll(inverse, back, 1)
        main = main - pltpu.roll(link * factor, stride, 1) - link * ahead
        right = right + pltpu.roll(factor * right, stride, 1) + ahead * pltpu.roll(right, back, 1)
        link = ahead * pltpu.roll(link, back, 1)
        stride *= 2
    solved[pl.ds(0, rows), :] = right / main


def sides(upper, own, got, last):
    pick = lambda a, b: jnp.where(upper, a, b)
    if not last:
        return [pick(g, o) for o, g in zip(own, got)], [pick(o, g) for o, g in zip(own, got)]
    zero = jnp.zeros_like(own[0])
    lower = [None, zero, pick(got[0], own[2]), None, pick(got[1], own[4])]
    higher = [pick(own[0], got[0]), zero, None, pick(own[3], got[1]), None]
    if len(own) > 5:
        lower += [None, pick(got[2], own[6])]
        higher += [pick(own[5], got[2]), None]
    return lower, higher


def join(lower, higher):
    if len(lower) == 5:
        return 1.0 / (lower[2] + higher[0]), None
    link = HALF_LINK * (lower[6] + higher[5])
    inverse = 1.0 / (1.0 + link * (lower[2] + higher[0]))
    return link * inverse, inverse


def is_upper(axis, level):
    return lax.rem(lax.div(lax.axis_index(axis), 1 << level), 2) == 1


def parts(ref, rows):
    if len(ref.shape) == 3:
        return [ref[k] for k in range(ref.shape[0])]
    return [ref[pl.ds(k * rows, rows), :] for k in range(ref.shape[0] // rows)]


def merge_kernel(axis, level, own, got, *outs):
    upper = is_upper(axis, level)
    size, rows = own.shape[:2]
    lower, higher = sides(upper, parts(own, rows), parts(got, rows), False)
    share, _ = join(lower, higher)
    gap = lower[4] - higher[3]
    first, second = share * lower[1], share * higher[1]
    merged = [
        lower[0] - first * lower[1],
        first * higher[1],
        higher[2] - second * higher[1],
        lower[3] - first * gap,
        higher[4] + second * gap,
        *([lower[5], higher[6]] if size > 5 else []),
    ]
    for k in range(size):
        outs[0][k] = merged[k]
    if len(outs) > 1:
        above = is_upper(axis, level + 1)
        for k, (high, low) in enumerate(LAST_SENT[: (size - 1) // 2]):
            outs[1][pl.ds(k * rows, rows), :] = jnp.where(above, merged[high], merged[low])


def unwind(axis, refs):
    rows = refs[0].shape[1]
    pairs = [parts(ref, rows) for ref in refs]
    zero = jnp.zeros_like(pairs[0][0])
    from_low = from_high = jump_low = jump_high = zero
    for level in range(len(pairs) // 2 - 1, -1, -1):
        upper = is_upper(axis, level)
        lower, higher = sides(upper, *pairs[2 * level : 2 * level + 2], level == len(pairs) // 2 - 1)
        share, inverse = join(lower, higher)
        gap = lower[4] - higher[3] + lower[1] * from_low - higher[1] * from_high
        flow = share * gap
        if inverse is not None:
            jump = inverse * gap
            jump_low, jump_high = jnp.where(upper, jump, jump_low), jnp.where(upper, jump_high, jump)
        from_low, from_high = jnp.where(upper, flow, from_low), jnp.where(upper, from_high, -flow)
    return from_low, from_high, jump_low, jump_high


def wide_sum_kernel(cut, height, slab, *refs):
    count = refs[-1].shape[0] // (cut * slab)
    along_x, (solved, head, tail), total = refs[:count], refs[count : count + 3], refs[-1]
    low, high, jump_low, jump_high = unwind("xy", refs[count + 3 : -1])

    def put(row, along_y):
        for k, piece in enumerate(along_x):
            at = pl.ds(k * cut * slab + row, cut, stride=slab)
            total[at, :] = piece[pl.ds(row, cut, stride=slab), :] + along_y[k * cut : (k + 1) * cut]

    for k in range(height):
        along_y = solved[k] + low * head[k] + high * tail[k]
        put(k, along_y)
        if k == 0:
            put(height, along_y + jump_low)
        if k == height - 1:
            put(height + 1, along_y - jump_high)


def sum_kernel(cut, height, *refs):
    count = refs[-1].shape[0] // (cut * height)
    along_x, (solved, head, tail), total = refs[:count], refs[count : count + 3], refs[-1]
    low, high, _, _ = unwind("xy", refs[count + 3 : -1])
    for row in range(height):
        along_y = solved[row] + low * head[row] + high * tail[row]
        for k, piece in enumerate(along_x):
            at = pl.ds(k * cut * height + row, cut, stride=height)
            total[at, :] = piece[pl.ds(row, cut, stride=height), :] + along_y[k * cut : (k + 1) * cut]


def step_kernel(depth, height, total, solved, head, tail, w_low, w_high, *refs):
    field, near, far, below, above = refs[-5:]
    slab = height + GHOSTS
    low, high, _, _ = unwind("gz", refs[:-5])
    for k in range(depth):
        along_z = solved[k] + low * head[k] + high * tail[k]
        value = (total[pl.ds(k * slab, slab), :] + along_z) * THIRD
        field[pl.ds(k * height, height), :] = value[:height]
        near[pl.ds(k, 1), :] = value[height : height + 1]
        far[pl.ds(k, 1), :] = value[height + 1 : height + 2]
        if k == 0:
            along_z = along_z + low / w_low[...]
            below[...] = (total[pl.ds(depth * slab, height), :] + along_z[:height]) * THIRD
        if k == depth - 1:
            along_z = solved[k] + low * head[k] + high * tail[k] + high / w_high[...]
            above[...] = (total[pl.ds((depth + 1) * slab, height), :] + along_z[:height]) * THIRD


def last_kernel(depth, height, total, solved, head, tail, slots, *refs):
    chunks = refs[-len(CHUNKS) :]
    low, high, _, _ = unwind("gz", refs[: -len(CHUNKS)])
    planes = BLOCK_ROWS // height
    for k in range(depth):
        value = (total[pl.ds(k * height, height), :] + (solved[k] + low * head[k] + high * tail[k])) * THIRD
        block, row, chunk = k // planes, (k % planes) * height, 0
        while row >= CHUNKS[chunk]:
            row, chunk = row - CHUNKS[chunk], chunk + 1
        chunks[chunk][pl.ds(block * CHUNKS[chunk] + row, height), :] = value
    chunks[0][pl.ds(depth // planes * CHUNKS[0], slots.shape[0]), :] = slots[...]


def pack_kernel(ways, number, sizes, *refs):
    pieces, outs = refs[: len(sizes)], refs[-ways:]
    slots, begin = (refs[0], number * sizes[0]) if len(refs) == len(sizes) + ways else (refs[len(sizes)], 0)
    me = lax.axis_index("gz")
    place = lax.rem(me, ways)
    placed = [jnp.max(slots[pl.ds(begin + block, 1), :]).astype(jnp.int32) for block in range(number)]
    for out in outs:
        out[...] = jnp.zeros_like(out)
    for block, slot in enumerate(placed):
        rank, target = lax.rem(slot, MOST), lax.div(slot, MOST) - (me - place)
        for way, out in enumerate(outs):

            @pl.when(target == lax.bitwise_xor(place, way))
            def _():
                row = 0
                for size, piece in zip(sizes, pieces):
                    out[rank, pl.ds(row, size), :] = piece[pl.ds(block * size, size), :]
                    row += size


def pack(ways, number, pieces, sizes, slots):
    shape = (MOST, sum(sizes), pieces[0].shape[1])
    return call(functools.partial(pack_kernel, ways, number, sizes), [shape] * ways, [*pieces, *slots])


def place_kernel(plan, kept, fresh, *refs):
    count = len(plan) + len(kept)
    outs, sems = refs[count + (not fresh) : -1], refs[-1]
    me = lax.axis_index("gz")
    moves, row = [], 0
    for k, (way, begin) in enumerate(plan):
        source = lax.bitwise_xor(me, way)
        rows = refs[k].shape[1]
        moves.append((refs[k], outs[0].at[pl.ds(source * MOST, MOST), pl.ds(begin, rows), :]))
    for size, ref in zip(kept, refs[len(plan) : count]):
        for block in range(outs[1].shape[0]):
            moves.append((ref.at[pl.ds(block * size, size), :], outs[1].at[block, pl.ds(row, size), :]))
        row += size
    copies = [pltpu.make_async_copy(*move, sems.at[k]) for k, move in enumerate(moves)]
    for copy in copies:
        copy.start()
    for copy in copies:
        copy.wait()


def place(arrays, plan, incoming, shapes, kept=()):
    count = len(arrays) + len(kept)
    copies = len(arrays) + len(kept) * (shapes[1][0] if kept else 0)
    extra = [] if incoming is None else [incoming]
    return pl.pallas_call(
        functools.partial(place_kernel, plan, CHUNKS if kept else (), not extra),
        out_shape=[jax.ShapeDtypeStruct(shape, jnp.float32) for shape in shapes],
        in_specs=[pl.BlockSpec(memory_space=VMEM)] * count + [pl.BlockSpec(memory_space=pl.ANY)] * len(extra),
        out_specs=[pl.BlockSpec(memory_space=pl.ANY)] * len(shapes),
        scratch_shapes=[pltpu.SemaphoreType.DMA((copies,))],
        input_output_aliases={count: 0} if extra else {},
        compiler_params=pltpu.CompilerParams(vmem_limit_bytes=VMEM_LIMIT),
    )(*arrays, *kept, *extra)


def swap(values, axis, stride):
    count = lax.axis_size(axis)
    return lax.ppermute(values, axis, [(i, i ^ stride) for i in range(count)])


def near(first, axis):
    return swap(first, axis, 1)


def far(second, axis):
    count = lax.axis_size(axis)
    if axis == "xy":
        other = [(i, (i + 1) % count) for i in range(1, count, 2)]
        return lax.ppermute(second, axis, other + [(j, i) for i, j in other])
    beside = lax.axis_size("xy")
    pairs = []
    for i in range(count):
        end = i in (0, count - 1)
        j = i if end else i + 1 if i % 2 else i - 1
        pairs += [(i * beside + c, j * beside + (c ^ 1 if end else c)) for c in range(beside)]
    return lax.ppermute(second, (axis, "xy"), pairs)


def neighbours(first, second, axis):
    got = far(second, axis)
    return near(first, axis), got


def merge(element, got, axis, level, after=()):
    size, rows, width = element.shape
    outs = [element.shape] + [((size - 1) // 2 * rows, width)] * (4 << level >= lax.axis_size(axis))
    merged = call(functools.partial(merge_kernel, axis, level), outs, [element, got], after=after)
    return merged[0], merged[-1]


def route(chunks, slots, number):
    count, width = lax.axis_size("gz"), chunks[0].shape[1]
    ways = count // 2
    order = range(ways - 1, 0, -1)
    crossed = []
    for chunk in chunks:
        crossed.append(swap(chunk, "gz", ways))
    straight = pack(ways, number, chunks, CHUNKS, [slots])
    arrays = [straight[0]]
    for way in order:
        arrays.append(swap(straight[way], "gz", way))
    shapes = [(count * MOST, BLOCK_ROWS, width), (number, BLOCK_ROWS, width)]
    plan = [(way, 0) for way in (0, *order)]
    incoming, field = place(arrays, plan, None, shapes, chunks)
    row = 0
    for k, size in enumerate(CHUNKS):
        others = [] if k == 0 else [lax.slice_in_dim(crossed[0], number * CHUNKS[0], None, axis=0)]
        passed = pack(ways, number, crossed[k : k + 1], (size,), others)
        arrays = [passed[0]]
        for way in order:
            arrays.append(swap(passed[way], "gz", way))
        plan = [(way ^ ways, row) for way in (0, *order)]
        (incoming,) = place(arrays, plan, incoming, shapes[:1])
        row += size
    return field, incoming


def lines(field, g_field, z_element, planes, height, slab, used, sum_body):
    width = field.shape[1]
    part = functools.partial
    z_rounds, y_rounds = (lax.axis_size(axis).bit_length() - 1 for axis in ("gz", "xy"))
    y_shape = (height, planes, width)
    *y_pieces, y_element = call(
        part(y_kernel, planes, height, slab),
        [y_shape, y_shape, y_shape, (7, planes, width)],
        [g_field, field],
        after=[z_element],
    )
    y_start, y_sent, y_pairs = y_element, y_element, []
    for level in range(y_rounds):
        y_pairs += [y_element, swap(y_sent, "xy", 1 << level)]
        if level + 1 < y_rounds:
            y_element, y_sent = merge(*y_pairs[-2:], "xy", level)
    cut, along_x = 8, []

    def x_part(after):
        k = len(along_x)
        rows = min(cut, used - k * cut) * slab
        along_x.extend(call(part(x_kernel, k * cut * slab, rows), [(cut * slab, width)], [g_field, field], after=after))

    z_sent, z_pairs = z_element, []
    for level in range(z_rounds):
        z_pairs += [z_element, swap(z_sent, "gz", 1 << level)]
        behind = []
        if level == 0:
            x_part([y_start])
            behind = [along_x[0], y_element]
        if level == 1:
            x_part([z_element])
            behind = [along_x[1]]
        if level == 2:
            while len(along_x) * cut < planes:
                x_part([z_element])
            (total,) = call(part(sum_body, cut), [(planes * slab, width)], [*along_x, *y_pieces, *y_pairs])
        if level + 1 < z_rounds:
            z_element, z_sent = merge(*z_pairs[-2:], "gz", level, behind)
    return total, z_pairs


def on_device(volume, owners):
    depth, height, width = volume.shape
    slab = height + GHOSTS
    planes = -(-(depth + 4) // 8) * 8
    blocks = owners.shape[1]
    part = functools.partial
    flat, plane, side = (depth * height, width), (height, width), (depth, width)

    field = volume.reshape(flat)
    edges = call(part(edge_kernel, depth, height), [(2 * depth, width)] * 2, [field])
    y_sides = neighbours(*edges, "xy")
    slabs, *edges = call(
        part(slab_kernel, depth, height), [(depth * slab, width)] + [(2 * slab, width)] * 2, [field, *y_sides]
    )
    z_sides = neighbours(*edges, "gz")
    slots = slots_of(owners, width, edges[0])
    field, g_field, *z_pieces, z_element, w_low, w_high = call(
        part(wide_kernel, depth, height),
        [(planes * slab, width)] * 2 + [(depth, slab, width)] * 3 + [(5, slab, width)] + [(slab, width)] * 2,
        [slabs, *z_sides],
        after=[slots],
    )
    total, z_pairs = lines(
        field, g_field, z_element, planes, height, slab, depth + 2, lambda cut, *refs: wide_sum_kernel(cut, height, slab, *refs)
    )
    field, *around = call(
        part(step_kernel, depth, height), [flat, side, side, plane, plane], [total, *z_pieces, w_low, w_high, *z_pairs]
    )
    g_field, *z_pieces, z_element = call(
        part(z_kernel, depth, height), [flat] + [(depth, height, width)] * 3 + [(7, height, width)], [field, *around]
    )
    total, z_pairs = lines(
        field, g_field, z_element, depth, height, height, depth, lambda cut, *refs: sum_kernel(cut, height, *refs)
    )
    rows = slots.shape[0]
    chunks = call(
        part(last_kernel, depth, height),
        [(blocks * size + rows * (k == 0), width) for k, size in enumerate(CHUNKS)],
        [total, *z_pieces, slots, *z_pairs],
    )
    field, incoming = route(chunks, slots, blocks)
    return field.reshape(volume.shape), incoming[None]


def solution(mesh):
    in_specs = (P("gz", "xy", None), P("xy", "gz", None))
    out_specs = (P("gz", "xy", None), P("xy", "gz", None, None))

    return jax.shard_map(on_device, mesh=mesh, in_specs=in_specs, out_specs=out_specs, check_vma=False)
```

```python
import functools

import jax
import jax.numpy as jnp
from jax import lax
from jax.experimental import pallas as pl
from jax.experimental.pallas import tpu as pltpu
from jax.sharding import PartitionSpec as P


MOST = 2
CHUNKS = (128,)
BLOCK_ROWS = 128
TIME_STEP = 30.0
CONTRAST = 4.0
HALF_LINK = 1.5 * TIME_STEP
THIRD = 1.0 / 3.0
GHOSTS = 8
LAST_SENT = ((0, 2), (3, 4), (5, 6))
VMEM_LIMIT = 16 * 1024 * 1024
VMEM = pltpu.VMEM


def call(body, outs, ins, after=()):
    count = len(ins)
    specs = [pl.BlockSpec(memory_space=VMEM)] * count + [pl.BlockSpec(memory_space=pl.ANY)] * len(after)
    return pl.pallas_call(
        lambda *refs: body(*refs[:count], *refs[count + len(after) :]),
        out_shape=[jax.ShapeDtypeStruct(shape, jnp.float32) for shape in outs],
        in_specs=specs,
        out_specs=[pl.BlockSpec(memory_space=VMEM)] * len(outs),
        compiler_params=pltpu.CompilerParams(vmem_limit_bytes=VMEM_LIMIT),
    )(*ins, *after)


def edge_kernel(depth, height, field, y_first, y_second):
    y_odd = lax.rem(lax.axis_index("xy"), 2) == 1
    for k in range(2):
        near = field[pl.ds(k, depth, stride=height), :]
        far = field[pl.ds(height - 1 - k, depth, stride=height), :]
        y_first[pl.ds(k * depth, depth), :] = jnp.where(y_odd, near, far)
        y_second[pl.ds(k * depth, depth), :] = jnp.where(y_odd, far, near)


def slab_kernel(depth, height, field, y_first, y_second, slabs, z_first, z_second):
    slab = height + GHOSTS
    y_odd = lax.rem(lax.axis_index("xy"), 2) == 1
    for k in range(depth):
        slabs[pl.ds(k * slab, height), :] = field[pl.ds(k * height, height), :]
    for k in range(2):
        one, two = y_first[pl.ds(k * depth, depth), :], y_second[pl.ds(k * depth, depth), :]
        slabs[pl.ds(height + 2 * k, depth, stride=slab), :] = jnp.where(y_odd, one, two)
        slabs[pl.ds(height + 2 * k + 1, depth, stride=slab), :] = jnp.where(y_odd, two, one)
    for k in range(4, GHOSTS):
        slabs[pl.ds(height + k, depth, stride=slab), :] = jnp.zeros((depth, field.shape[1]), field.dtype)
    z_odd = lax.rem(lax.axis_index("gz"), 2) == 1
    for k in range(2):
        low, high = slabs[pl.ds(k * slab, slab), :], slabs[pl.ds((depth - 1 - k) * slab, slab), :]
        z_first[pl.ds(k * slab, slab), :] = jnp.where(z_odd, low, high)
        z_second[pl.ds(k * slab, slab), :] = jnp.where(z_odd, high, low)


def slot_kernel(given, first, slots, owners, sem):
    copy = pltpu.make_async_copy(given, owners, sem)
    copy.start()
    slots[...] = jnp.zeros_like(slots)
    copy.wait()
    for block in range(owners.shape[1]):
        rank = jnp.int32(0)
        for other in range(block):
            rank = rank + (owners[0, other] == owners[0, block]).astype(jnp.int32)
        slot = owners[0, block] * MOST + rank
        slots[pl.ds(block, 1), :] = jnp.full((1, slots.shape[1]), slot.astype(jnp.float32))


def slots_of(owners, width, after):
    blocks = owners.shape[1]
    return pl.pallas_call(
        slot_kernel,
        out_shape=jax.ShapeDtypeStruct((-(-blocks // 8) * 8, width), jnp.float32),
        in_specs=[pl.BlockSpec(memory_space=pl.ANY)] * 2,
        out_specs=pl.BlockSpec(memory_space=VMEM),
        scratch_shapes=[pltpu.SMEM((1, blocks), jnp.int32), pltpu.SemaphoreType.DMA],
        compiler_params=pltpu.CompilerParams(vmem_limit_bytes=VMEM_LIMIT),
        name="slots",
    )(owners.reshape(1, blocks), after)


def chain(g_rows, v_rows, count, solved, head, tail, element):
    g_head = g_prev = g_rows(0)
    pivot = jnp.ones_like(g_prev)
    right = v_rows(0)
    unit = pivot
    for k in range(count - 1):
        g_next = g_rows(k + 1)
        link = HALF_LINK * (g_prev + g_next)
        inverse = 1.0 / (pivot + link)
        ratio = link * inverse
        solved[k] = right * inverse
        head[k] = unit * inverse
        tail[k] = ratio
        pivot = 1.0 + ratio * pivot
        right = v_rows(k + 1) + ratio * right
        unit = ratio * unit
        g_prev = g_next
    inverse = 1.0 / pivot
    value, from_head, from_tail = right * inverse, unit * inverse, inverse
    solved[count - 1] = value
    head[count - 1] = from_head
    tail[count - 1] = from_tail
    element[2] = from_tail
    element[4] = value
    if element.shape[0] > 5:
        element[5] = g_head
        element[6] = g_prev
    for k in range(count - 2, -1, -1):
        ratio = tail[k]
        value = solved[k] + ratio * value
        from_head = head[k] + ratio * from_head
        from_tail = ratio * from_tail
        solved[k] = value
        head[k] = from_head
        tail[k] = from_tail
    element[0] = from_head
    element[1] = from_tail
    element[3] = value


def diffusivity(up, down, after, before, right, left):
    squares = ((up - down) * 0.5) * ((up - down) * 0.5)
    slope = (after - before) * 0.5
    squares = squares + slope * slope
    slope = (right - left) * 0.5
    squares = squares + slope * slope
    return 1.0 / (1.0 + squares * (1.0 / CONTRAST))


def x_sides(here):
    width = here.shape[1]
    lanes = lax.broadcasted_iota(jnp.int32, here.shape, 1)
    right = jnp.where(lanes == width - 1, here, pltpu.roll(here, width - 1, 1))
    return right, jnp.where(lanes == 0, here, pltpu.roll(here, 1, 1))


def ends(axis):
    index = lax.axis_index(axis)
    return index == 0, index == lax.axis_size(axis) - 1


def wide_kernel(depth, height, slabs, z_first, z_second, field, g_out, solved, head, tail, element, w_low, w_high, sent):
    slab = height + GHOSTS
    width = slabs.shape[1]
    z_odd = lax.rem(lax.axis_index("gz"), 2) == 1
    z_begin, z_end = ends("gz")
    y_begin, y_end = ends("xy")
    rows = lax.broadcasted_iota(jnp.int32, (slab, width), 0)
    own = depth * slab
    field[pl.ds(0, own), :] = slabs[...]
    for k in range(2):
        one, two = z_first[pl.ds(k * slab, slab), :], z_second[pl.ds(k * slab, slab), :]
        field[pl.ds(own + 2 * k * slab, slab), :] = jnp.where(z_odd, one, two)
        field[pl.ds(own + (2 * k + 1) * slab, slab), :] = jnp.where(z_odd, two, one)
    spare = field.shape[0] - own - 4 * slab
    field[pl.ds(own + 4 * slab, spare), :] = jnp.zeros((spare, width), field.dtype)
    g_out[pl.ds(own + 2 * slab, spare + 2 * slab), :] = jnp.ones((spare + 2 * slab, width), field.dtype)

    def begin(k):
        if k < 0:
            return own + (2 if k < -1 else 0) * slab
        return own + (1 + 2 * (k - depth)) * slab if k >= depth else k * slab

    plane = lambda k: field[pl.ds(begin(k), slab), :]

    def g_rows(k):
        here, up, down = plane(k), plane(k + 1), plane(k - 1)
        if k == 0:
            down = jnp.where(z_begin, here, down)
        if k == depth - 1:
            up = jnp.where(z_end, here, up)
        row = lambda r: field[pl.ds(begin(k) + r, 1), :]
        first, final = row(0), row(height - 1)
        after = jnp.where(rows == height - 1, jnp.where(y_end, final, row(height + 1)), pltpu.roll(here, slab - 1, 0))
        after = jnp.where(rows == height, first, jnp.where(rows == height + 1, row(height + 3), after))
        before = jnp.where(rows == 0, jnp.where(y_begin, first, row(height)), pltpu.roll(here, 1, 0))
        before = jnp.where(rows == height, row(height + 2), jnp.where(rows == height + 1, final, before))
        g = diffusivity(up, down, after, before, *x_sides(here))
        g_out[pl.ds(begin(k), slab), :] = g
        return g

    chain(g_rows, plane, depth, solved, head, tail, element)
    g_own = lambda k: g_out[pl.ds(k * slab, slab), :]
    w_low[...] = HALF_LINK * (g_own(0) + g_rows(-1))
    link = HALF_LINK * (g_own(depth - 1) + g_rows(depth))
    w_high[...] = link
    element[2] = element[2] + 1.0 / link
    put(sent, [element[k] for k in range(5)], True)


def z_kernel(depth, height, field, near, far, low, high, g_out, solved, head, tail, element):
    plane = lambda k: field[pl.ds(k * height, height), :]
    z_begin, z_end = ends("gz")
    y_begin, y_end = ends("xy")
    below = jnp.where(z_begin, plane(0), low[...])
    above = jnp.where(z_end, plane(depth - 1), high[...])
    rows = lax.broadcasted_iota(jnp.int32, (height, field.shape[1]), 0)

    def g_rows(k):
        here = plane(k)
        up, down = plane(k + 1) if k < depth - 1 else above, plane(k - 1) if k else below
        first = jnp.where(y_begin, here[:1], near[pl.ds(k, 1), :])
        final = jnp.where(y_end, here[height - 1 :], far[pl.ds(k, 1), :])
        after = jnp.where(rows == height - 1, final, pltpu.roll(here, height - 1, 0))
        before = jnp.where(rows == 0, first, pltpu.roll(here, 1, 0))
        g = diffusivity(up, down, after, before, *x_sides(here))
        g_out[pl.ds(k * height, height), :] = g
        return g

    chain(g_rows, plane, depth, solved, head, tail, element)


def y_kernel(planes, height, slab, g_field, field, solved, head, tail, element):
    g_rows = lambda k: g_field[pl.ds(k, planes, stride=slab), :]
    v_rows = lambda k: field[pl.ds(k, planes, stride=slab), :]
    chain(g_rows, v_rows, height, solved, head, tail, element)


def x_kernel(first, rows, g_field, field, solved):
    width = field.shape[1]
    at = pl.ds(first, rows)
    g, right = g_field[at, :], field[at, :]
    lanes = lax.broadcasted_iota(jnp.int32, (rows, width), 1)
    link = jnp.where(lanes == width - 1, 0.0, HALF_LINK * (g + pltpu.roll(g, width - 1, 1)))
    main = 1.0 + link + pltpu.roll(link, 1, 1)
    stride = 1
    while stride < width:
        inverse = 1.0 / main
        factor = link * inverse
        back = width - stride
        ahead = link * pltpu.roll(inverse, back, 1)
        main = main - pltpu.roll(link * factor, stride, 1) - link * ahead
        right = right + pltpu.roll(factor * right, stride, 1) + ahead * pltpu.roll(right, back, 1)
        link = ahead * pltpu.roll(link, back, 1)
        stride *= 2
    solved[pl.ds(0, rows), :] = right / main


def sides(upper, own, got, last):
    pick = lambda a, b: jnp.where(upper, a, b)
    if not last:
        return [pick(g, o) for o, g in zip(own, got)], [pick(o, g) for o, g in zip(own, got)]
    zero = jnp.zeros_like(own[0])
    lower = [None, zero, pick(got[0], own[2]), None, pick(got[1], own[4])]
    higher = [pick(own[0], got[0]), zero, None, pick(own[3], got[1]), None]
    if len(own) > 5:
        lower += [None, pick(got[2], own[6])]
        higher += [pick(own[5], got[2]), None]
    return lower, higher


def join(lower, higher):
    if len(lower) == 5:
        return 1.0 / (lower[2] + higher[0]), None
    link = HALF_LINK * (lower[6] + higher[5])
    inverse = 1.0 / (1.0 + link * (lower[2] + higher[0]))
    return link * inverse, inverse


def is_upper(axis, level):
    return lax.rem(lax.div(lax.axis_index(axis), 1 << level), 2) == 1


def packed(count, rows, wide):
    return count * (rows - GHOSTS) + -(-2 * count // 8) * 8 if wide else count * rows


def put(ref, values, wide):
    rows = values[0].shape[0] - GHOSTS * wide
    for k, value in enumerate(values):
        ref[pl.ds(k * rows, rows), :] = value[:rows]
        if wide:
            ref[pl.ds(len(values) * rows + 2 * k, 2), :] = value[rows : rows + 2]


def parts(ref, rows, wide):
    if len(ref.shape) == 3:
        return [ref[k] for k in range(ref.shape[0])]
    rows -= GHOSTS * wide
    count = ref.shape[0] // rows
    values = [ref[pl.ds(k * rows, rows), :] for k in range(count)]
    if wide:
        for k in range(count):
            begin = count * rows + 2 * k
            fitting = min(begin, ref.shape[0] - 8)
            ghosts = ref[pl.ds(fitting, 8), :]
            if begin > fitting:
                ghosts = pltpu.roll(ghosts, 8 - begin + fitting, 0)
            values[k] = jnp.concatenate([values[k], ghosts], axis=0)
    return values


def merge_kernel(axis, level, last, own, got, *outs):
    upper = is_upper(axis, level)
    size, rows = own.shape[:2]
    wide = size == 5
    lower, higher = sides(upper, parts(own, rows, wide), parts(got, rows, wide), False)
    share, _ = join(lower, higher)
    gap = lower[4] - higher[3]
    first, second = share * lower[1], share * higher[1]
    merged = [
        lower[0] - first * lower[1],
        first * higher[1],
        higher[2] - second * higher[1],
        lower[3] - first * gap,
        higher[4] + second * gap,
        *([] if wide else [lower[5], higher[6]]),
    ]
    for k in range(size):
        outs[0][k] = merged[k]
    if len(outs) > 1:
        above = is_upper(axis, level + 1)
        sent = [jnp.where(above, merged[high], merged[low]) for high, low in LAST_SENT[: (size - 1) // 2]]
        put(outs[1], sent if last else merged, wide)


def unwind(axis, refs):
    rows = refs[0].shape[1]
    pairs = [parts(ref, rows, refs[0].shape[0] == 5) for ref in refs]
    zero = jnp.zeros_like(pairs[0][0])
    from_low = from_high = jump_low = jump_high = zero
    for level in range(len(pairs) // 2 - 1, -1, -1):
        upper = is_upper(axis, level)
        lower, higher = sides(upper, *pairs[2 * level : 2 * level + 2], level == len(pairs) // 2 - 1)
        share, inverse = join(lower, higher)
        gap = lower[4] - higher[3] + lower[1] * from_low - higher[1] * from_high
        flow = share * gap
        if inverse is not None:
            jump = inverse * gap
            jump_low, jump_high = jnp.where(upper, jump, jump_low), jnp.where(upper, jump_high, jump)
        from_low, from_high = jnp.where(upper, flow, from_low), jnp.where(upper, from_high, -flow)
    return from_low, from_high, jump_low, jump_high


def wide_sum_kernel(cut, height, slab, *refs):
    count = refs[-1].shape[0] // (cut * slab)
    along_x, (solved, head, tail), total = refs[:count], refs[count : count + 3], refs[-1]
    low, high, jump_low, jump_high = unwind("xy", refs[count + 3 : -1])

    def put(row, along_y):
        for k, piece in enumerate(along_x):
            at = pl.ds(k * cut * slab + row, cut, stride=slab)
            total[at, :] = piece[pl.ds(row, cut, stride=slab), :] + along_y[k * cut : (k + 1) * cut]

    for k in range(height):
        along_y = solved[k] + low * head[k] + high * tail[k]
        put(k, along_y)
        if k == 0:
            put(height, along_y + jump_low)
        if k == height - 1:
            put(height + 1, along_y - jump_high)


def sum_kernel(cut, height, *refs):
    count = refs[-1].shape[0] // (cut * height)
    along_x, (solved, head, tail), total = refs[:count], refs[count : count + 3], refs[-1]
    low, high, _, _ = unwind("xy", refs[count + 3 : -1])
    for row in range(height):
        along_y = solved[row] + low * head[row] + high * tail[row]
        for k, piece in enumerate(along_x):
            at = pl.ds(k * cut * height + row, cut, stride=height)
            total[at, :] = piece[pl.ds(row, cut, stride=height), :] + along_y[k * cut : (k + 1) * cut]


def step_kernel(depth, height, total, solved, head, tail, w_low, w_high, *refs):
    field, near, far, below, above = refs[-5:]
    slab = height + GHOSTS
    low, high, _, _ = unwind("gz", refs[:-5])
    for k in range(depth):
        along_z = solved[k] + low * head[k] + high * tail[k]
        value = (total[pl.ds(k * slab, slab), :] + along_z) * THIRD
        field[pl.ds(k * height, height), :] = value[:height]
        near[pl.ds(k, 1), :] = value[height : height + 1]
        far[pl.ds(k, 1), :] = value[height + 1 : height + 2]
        if k == 0:
            along_z = along_z + low / w_low[...]
            below[...] = (total[pl.ds(depth * slab, height), :] + along_z[:height]) * THIRD
        if k == depth - 1:
            along_z = solved[k] + low * head[k] + high * tail[k] + high / w_high[...]
            above[...] = (total[pl.ds((depth + 1) * slab, height), :] + along_z[:height]) * THIRD


def last_kernel(depth, height, total, solved, head, tail, slots, *refs):
    chunks = refs[-len(CHUNKS) :]
    low, high, _, _ = unwind("gz", refs[: -len(CHUNKS)])
    planes = BLOCK_ROWS // height
    for k in range(depth):
        value = (total[pl.ds(k * height, height), :] + (solved[k] + low * head[k] + high * tail[k])) * THIRD
        block, row, chunk = k // planes, (k % planes) * height, 0
        while row >= CHUNKS[chunk]:
            row, chunk = row - CHUNKS[chunk], chunk + 1
        chunks[chunk][pl.ds(block * CHUNKS[chunk] + row, height), :] = value
    chunks[0][pl.ds(depth // planes * CHUNKS[0], slots.shape[0]), :] = slots[...]


def pack_kernel(ways, number, sizes, *refs):
    pieces, outs = refs[: len(sizes)], refs[-ways:]
    slots, begin = (refs[0], number * sizes[0]) if len(refs) == len(sizes) + ways else (refs[len(sizes)], 0)
    me = lax.axis_index("gz")
    place = lax.rem(me, ways)
    placed = [jnp.max(slots[pl.ds(begin + block, 1), :]).astype(jnp.int32) for block in range(number)]
    for out in outs:
        out[...] = jnp.zeros_like(out)
    for block, slot in enumerate(placed):
        rank, target = lax.rem(slot, MOST), lax.div(slot, MOST) - (me - place)
        for way, out in enumerate(outs):

            @pl.when(target == lax.bitwise_xor(place, way))
            def _():
                row = 0
                for size, piece in zip(sizes, pieces):
                    out[rank, pl.ds(row, size), :] = piece[pl.ds(block * size, size), :]
                    row += size


def pack(ways, number, pieces, sizes, slots):
    shape = (MOST, sum(sizes), pieces[0].shape[1])
    return call(functools.partial(pack_kernel, ways, number, sizes), [shape] * ways, [*pieces, *slots])


def place_kernel(plan, kept, fresh, *refs):
    count = len(plan) + len(kept)
    outs, sems = refs[count + (not fresh) : -1], refs[-1]
    me = lax.axis_index("gz")
    moves, row = [], 0
    for k, (way, begin) in enumerate(plan):
        source = lax.bitwise_xor(me, way)
        rows = refs[k].shape[1]
        moves.append((refs[k], outs[0].at[pl.ds(source * MOST, MOST), pl.ds(begin, rows), :]))
    for size, ref in zip(kept, refs[len(plan) : count]):
        for block in range(outs[1].shape[0]):
            moves.append((ref.at[pl.ds(block * size, size), :], outs[1].at[block, pl.ds(row, size), :]))
        row += size
    copies = [pltpu.make_async_copy(*move, sems.at[k]) for k, move in enumerate(moves)]
    for copy in copies:
        copy.start()
    for copy in copies:
        copy.wait()


def place(arrays, plan, incoming, shapes, kept=()):
    count = len(arrays) + len(kept)
    copies = len(arrays) + len(kept) * (shapes[1][0] if kept else 0)
    extra = [] if incoming is None else [incoming]
    return pl.pallas_call(
        functools.partial(place_kernel, plan, CHUNKS if kept else (), not extra),
        out_shape=[jax.ShapeDtypeStruct(shape, jnp.float32) for shape in shapes],
        in_specs=[pl.BlockSpec(memory_space=VMEM)] * count + [pl.BlockSpec(memory_space=pl.ANY)] * len(extra),
        out_specs=[pl.BlockSpec(memory_space=pl.ANY)] * len(shapes),
        scratch_shapes=[pltpu.SemaphoreType.DMA((copies,))],
        input_output_aliases={count: 0} if extra else {},
        compiler_params=pltpu.CompilerParams(vmem_limit_bytes=VMEM_LIMIT),
    )(*arrays, *kept, *extra)


def swap(values, axis, stride):
    count = lax.axis_size(axis)
    return lax.ppermute(values, axis, [(i, i ^ stride) for i in range(count)])


def near(first, axis):
    return swap(first, axis, 1)


def far(second, axis):
    count = lax.axis_size(axis)
    if axis == "xy":
        other = [(i, (i + 1) % count) for i in range(1, count, 2)]
        return lax.ppermute(second, axis, other + [(j, i) for i, j in other])
    beside = lax.axis_size("xy")
    pairs = []
    for i in range(count):
        end = i in (0, count - 1)
        j = i if end else i + 1 if i % 2 else i - 1
        pairs += [(i * beside + c, j * beside + (c ^ 1 if end else c)) for c in range(beside)]
    return lax.ppermute(second, (axis, "xy"), pairs)


def neighbours(first, second, axis):
    got = far(second, axis)
    return near(first, axis), got


def merge(element, got, axis, level, after=()):
    size, rows, width = element.shape
    last, wide = 4 << level >= lax.axis_size(axis), size == 5
    count = (size - 1) // 2 if last else size
    outs = [element.shape] + [(packed(count, rows, wide), width)] * (last or wide)
    merged = call(functools.partial(merge_kernel, axis, level, last), outs, [element, got], after=after)
    return merged[0], merged[-1]


def route(chunks, slots, number):
    count, width = lax.axis_size("gz"), chunks[0].shape[1]
    ways = count // 2
    order = range(ways - 1, 0, -1)
    crossed = []
    for chunk in chunks:
        crossed.append(swap(chunk, "gz", ways))
    straight = pack(ways, number, chunks, CHUNKS, [slots])
    arrays = [straight[0]]
    for way in order:
        arrays.append(swap(straight[way], "gz", way))
    shapes = [(count * MOST, BLOCK_ROWS, width), (number, BLOCK_ROWS, width)]
    plan = [(way, 0) for way in (0, *order)]
    incoming, field = place(arrays, plan, None, shapes, chunks)
    row = 0
    for k, size in enumerate(CHUNKS):
        others = [] if k == 0 else [lax.slice_in_dim(crossed[0], number * CHUNKS[0], None, axis=0)]
        passed = pack(ways, number, crossed[k : k + 1], (size,), others)
        arrays = [passed[0]]
        for way in order:
            arrays.append(swap(passed[way], "gz", way))
        plan = [(way ^ ways, row) for way in (0, *order)]
        (incoming,) = place(arrays, plan, incoming, shapes[:1])
        row += size
    return field, incoming


def lines(field, g_field, z_element, z_sent, planes, height, slab, used, sum_body):
    width = field.shape[1]
    part = functools.partial
    z_rounds, y_rounds = (lax.axis_size(axis).bit_length() - 1 for axis in ("gz", "xy"))
    y_shape = (height, planes, width)
    *y_pieces, y_element = call(
        part(y_kernel, planes, height, slab),
        [y_shape, y_shape, y_shape, (7, planes, width)],
        [g_field, field],
        after=[z_element],
    )
    y_start, y_sent, y_pairs = y_element, y_element, []
    for level in range(y_rounds):
        y_pairs += [y_element, swap(y_sent, "xy", 1 << level)]
        if level + 1 < y_rounds:
            y_element, y_sent = merge(*y_pairs[-2:], "xy", level)
    cut, along_x = 8, []

    def x_part(after):
        k = len(along_x)
        rows = min(cut, used - k * cut) * slab
        along_x.extend(call(part(x_kernel, k * cut * slab, rows), [(cut * slab, width)], [g_field, field], after=after))

    z_pairs = []
    for level in range(z_rounds):
        z_pairs += [z_element, swap(z_sent, "gz", 1 << level)]
        behind = []
        if level == 0:
            x_part([y_start])
            behind = [along_x[0], y_element]
        if level == 1:
            x_part([z_element])
            behind = [along_x[1]]
        if level == 2:
            while len(along_x) * cut < planes:
                x_part([z_element])
            (total,) = call(part(sum_body, cut), [(planes * slab, width)], [*along_x, *y_pieces, *y_pairs])
        if level + 1 < z_rounds:
            z_element, z_sent = merge(*z_pairs[-2:], "gz", level, behind)
    return total, z_pairs


def on_device(volume, owners):
    depth, height, width = volume.shape
    slab = height + GHOSTS
    planes = -(-(depth + 4) // 8) * 8
    blocks = owners.shape[1]
    part = functools.partial
    flat, plane, side = (depth * height, width), (height, width), (depth, width)

    field = volume.reshape(flat)
    edges = call(part(edge_kernel, depth, height), [(2 * depth, width)] * 2, [field])
    y_sides = neighbours(*edges, "xy")
    slabs, *edges = call(
        part(slab_kernel, depth, height), [(depth * slab, width)] + [(2 * slab, width)] * 2, [field, *y_sides]
    )
    z_sides = neighbours(*edges, "gz")
    slots = slots_of(owners, width, edges[0])
    field, g_field, *z_pieces, z_element, w_low, w_high, z_sent = call(
        part(wide_kernel, depth, height),
        [(planes * slab, width)] * 2 + [(depth, slab, width)] * 3 + [(5, slab, width)] + [(slab, width)] * 2 + [(packed(5, slab, True), width)],
        [slabs, *z_sides],
        after=[slots],
    )
    total, z_pairs = lines(
        field, g_field, z_element, z_sent, planes, height, slab, depth + 2, lambda cut, *refs: wide_sum_kernel(cut, height, slab, *refs)
    )
    field, *around = call(
        part(step_kernel, depth, height), [flat, side, side, plane, plane], [total, *z_pieces, w_low, w_high, *z_pairs]
    )
    g_field, *z_pieces, z_element = call(
        part(z_kernel, depth, height), [flat] + [(depth, height, width)] * 3 + [(7, height, width)], [field, *around]
    )
    total, z_pairs = lines(
        field, g_field, z_element, z_element, depth, height, height, depth, lambda cut, *refs: sum_kernel(cut, height, *refs)
    )
    rows = slots.shape[0]
    chunks = call(
        part(last_kernel, depth, height),
        [(blocks * size + rows * (k == 0), width) for k, size in enumerate(CHUNKS)],
        [total, *z_pieces, slots, *z_pairs],
    )
    field, incoming = route(chunks, slots, blocks)
    return field.reshape(volume.shape), incoming[None]


def solution(mesh):
    in_specs = (P("gz", "xy", None), P("xy", "gz", None))
    out_specs = (P("gz", "xy", None), P("xy", "gz", None, None))

    return jax.shard_map(on_device, mesh=mesh, in_specs=in_specs, out_specs=out_specs, check_vma=False)
```

```python
import functools

import jax
import jax.numpy as jnp
from jax import lax
from jax.experimental import pallas as pl
from jax.experimental.pallas import tpu as pltpu
from jax.sharding import PartitionSpec as P


MOST = 2
CHUNKS = (128,)
BLOCK_ROWS = 128
TIME_STEP = 30.0
CONTRAST = 4.0
HALF_LINK = 1.5 * TIME_STEP
THIRD = 1.0 / 3.0
GHOSTS = 8
LAST_SENT = ((0, 2), (3, 4), (5, 6))
VMEM_LIMIT = 16 * 1024 * 1024
VMEM = pltpu.VMEM


def call(body, outs, ins, after=()):
    count = len(ins)
    specs = [pl.BlockSpec(memory_space=VMEM)] * count + [pl.BlockSpec(memory_space=pl.ANY)] * len(after)
    return pl.pallas_call(
        lambda *refs: body(*refs[:count], *refs[count + len(after) :]),
        out_shape=[jax.ShapeDtypeStruct(shape, jnp.float32) for shape in outs],
        in_specs=specs,
        out_specs=[pl.BlockSpec(memory_space=VMEM)] * len(outs),
        compiler_params=pltpu.CompilerParams(vmem_limit_bytes=VMEM_LIMIT),
    )(*ins, *after)


def edge_kernel(depth, height, field, y_first, y_second):
    y_odd = lax.rem(lax.axis_index("xy"), 2) == 1
    for k in range(2):
        near = field[pl.ds(k, depth, stride=height), :]
        far = field[pl.ds(height - 1 - k, depth, stride=height), :]
        y_first[pl.ds(k * depth, depth), :] = jnp.where(y_odd, near, far)
        y_second[pl.ds(k * depth, depth), :] = jnp.where(y_odd, far, near)


def slab_kernel(depth, height, field, y_first, y_second, slabs, z_first, z_second):
    slab = height + GHOSTS
    y_odd = lax.rem(lax.axis_index("xy"), 2) == 1
    for k in range(depth):
        slabs[pl.ds(k * slab, height), :] = field[pl.ds(k * height, height), :]
    for k in range(2):
        one, two = y_first[pl.ds(k * depth, depth), :], y_second[pl.ds(k * depth, depth), :]
        slabs[pl.ds(height + 2 * k, depth, stride=slab), :] = jnp.where(y_odd, one, two)
        slabs[pl.ds(height + 2 * k + 1, depth, stride=slab), :] = jnp.where(y_odd, two, one)
    for k in range(4, GHOSTS):
        slabs[pl.ds(height + k, depth, stride=slab), :] = jnp.zeros((depth, field.shape[1]), field.dtype)
    z_odd = lax.rem(lax.axis_index("gz"), 2) == 1
    for k in range(2):
        low, high = slabs[pl.ds(k * slab, slab), :], slabs[pl.ds((depth - 1 - k) * slab, slab), :]
        z_first[pl.ds(k * slab, slab), :] = jnp.where(z_odd, low, high)
        z_second[pl.ds(k * slab, slab), :] = jnp.where(z_odd, high, low)


def slot_kernel(given, first, slots, owners, sem):
    copy = pltpu.make_async_copy(given, owners, sem)
    copy.start()
    slots[...] = jnp.zeros_like(slots)
    copy.wait()
    for block in range(owners.shape[1]):
        rank = jnp.int32(0)
        for other in range(block):
            rank = rank + (owners[0, other] == owners[0, block]).astype(jnp.int32)
        slot = owners[0, block] * MOST + rank
        slots[pl.ds(block, 1), :] = jnp.full((1, slots.shape[1]), slot.astype(jnp.float32))


def slots_of(owners, width, after):
    blocks = owners.shape[1]
    return pl.pallas_call(
        slot_kernel,
        out_shape=jax.ShapeDtypeStruct((-(-blocks // 8) * 8, width), jnp.float32),
        in_specs=[pl.BlockSpec(memory_space=pl.ANY)] * 2,
        out_specs=pl.BlockSpec(memory_space=VMEM),
        scratch_shapes=[pltpu.SMEM((1, blocks), jnp.int32), pltpu.SemaphoreType.DMA],
        compiler_params=pltpu.CompilerParams(vmem_limit_bytes=VMEM_LIMIT),
        name="slots",
    )(owners.reshape(1, blocks), after)


def chain(g_rows, v_rows, count, solved, head, tail, element):
    g_head = g_prev = g_rows(0)
    pivot = jnp.ones_like(g_prev)
    right = v_rows(0)
    unit = pivot
    for k in range(count - 1):
        g_next = g_rows(k + 1)
        link = HALF_LINK * (g_prev + g_next)
        inverse = 1.0 / (pivot + link)
        ratio = link * inverse
        solved[k] = right * inverse
        head[k] = unit * inverse
        tail[k] = ratio
        pivot = 1.0 + ratio * pivot
        right = v_rows(k + 1) + ratio * right
        unit = ratio * unit
        g_prev = g_next
    inverse = 1.0 / pivot
    value, from_head, from_tail = right * inverse, unit * inverse, inverse
    solved[count - 1] = value
    head[count - 1] = from_head
    tail[count - 1] = from_tail
    element[2] = from_tail
    element[4] = value
    if element.shape[0] > 5:
        element[5] = g_head
        element[6] = g_prev
    for k in range(count - 2, -1, -1):
        ratio = tail[k]
        value = solved[k] + ratio * value
        from_head = head[k] + ratio * from_head
        from_tail = ratio * from_tail
        solved[k] = value
        head[k] = from_head
        tail[k] = from_tail
    element[0] = from_head
    element[1] = from_tail
    element[3] = value


def diffusivity(up, down, after, before, right, left):
    squares = ((up - down) * 0.5) * ((up - down) * 0.5)
    slope = (after - before) * 0.5
    squares = squares + slope * slope
    slope = (right - left) * 0.5
    squares = squares + slope * slope
    return 1.0 / (1.0 + squares * (1.0 / CONTRAST))


def x_sides(here):
    width = here.shape[1]
    lanes = lax.broadcasted_iota(jnp.int32, here.shape, 1)
    right = jnp.where(lanes == width - 1, here, pltpu.roll(here, width - 1, 1))
    return right, jnp.where(lanes == 0, here, pltpu.roll(here, 1, 1))


def ends(axis):
    index = lax.axis_index(axis)
    return index == 0, index == lax.axis_size(axis) - 1


def wide_kernel(depth, height, slabs, z_first, z_second, field, g_out, solved, head, tail, element, w_low, w_high, sent):
    slab = height + GHOSTS
    width = slabs.shape[1]
    z_odd = lax.rem(lax.axis_index("gz"), 2) == 1
    z_begin, z_end = ends("gz")
    y_begin, y_end = ends("xy")
    rows = lax.broadcasted_iota(jnp.int32, (slab, width), 0)
    own = depth * slab
    field[pl.ds(0, own), :] = slabs[...]
    for k in range(2):
        one, two = z_first[pl.ds(k * slab, slab), :], z_second[pl.ds(k * slab, slab), :]
        field[pl.ds(own + 2 * k * slab, slab), :] = jnp.where(z_odd, one, two)
        field[pl.ds(own + (2 * k + 1) * slab, slab), :] = jnp.where(z_odd, two, one)
    spare = field.shape[0] - own - 4 * slab
    field[pl.ds(own + 4 * slab, spare), :] = jnp.zeros((spare, width), field.dtype)
    g_out[pl.ds(own + 2 * slab, spare + 2 * slab), :] = jnp.ones((spare + 2 * slab, width), field.dtype)

    def begin(k):
        if k < 0:
            return own + (2 if k < -1 else 0) * slab
        return own + (1 + 2 * (k - depth)) * slab if k >= depth else k * slab

    plane = lambda k: field[pl.ds(begin(k), slab), :]

    def g_rows(k):
        here, up, down = plane(k), plane(k + 1), plane(k - 1)
        if k == 0:
            down = jnp.where(z_begin, here, down)
        if k == depth - 1:
            up = jnp.where(z_end, here, up)
        row = lambda r: field[pl.ds(begin(k) + r, 1), :]
        first, final = row(0), row(height - 1)
        after = jnp.where(rows == height - 1, jnp.where(y_end, final, row(height + 1)), pltpu.roll(here, slab - 1, 0))
        after = jnp.where(rows == height, first, jnp.where(rows == height + 1, row(height + 3), after))
        before = jnp.where(rows == 0, jnp.where(y_begin, first, row(height)), pltpu.roll(here, 1, 0))
        before = jnp.where(rows == height, row(height + 2), jnp.where(rows == height + 1, final, before))
        g = diffusivity(up, down, after, before, *x_sides(here))
        g_out[pl.ds(begin(k), slab), :] = g
        return g

    chain(g_rows, plane, depth, solved, head, tail, element)
    g_own = lambda k: g_out[pl.ds(k * slab, slab), :]
    w_low[...] = HALF_LINK * (g_own(0) + g_rows(-1))
    link = HALF_LINK * (g_own(depth - 1) + g_rows(depth))
    w_high[...] = link
    element[2] = element[2] + 1.0 / link
    put(sent, [element[k] for k in range(5)], True)


def z_kernel(depth, height, field, near, far, low, high, g_out, solved, head, tail, element):
    plane = lambda k: field[pl.ds(k * height, height), :]
    z_begin, z_end = ends("gz")
    y_begin, y_end = ends("xy")
    below = jnp.where(z_begin, plane(0), low[...])
    above = jnp.where(z_end, plane(depth - 1), high[...])
    rows = lax.broadcasted_iota(jnp.int32, (height, field.shape[1]), 0)

    def g_rows(k):
        here = plane(k)
        up, down = plane(k + 1) if k < depth - 1 else above, plane(k - 1) if k else below
        first = jnp.where(y_begin, here[:1], near[pl.ds(k, 1), :])
        final = jnp.where(y_end, here[height - 1 :], far[pl.ds(k, 1), :])
        after = jnp.where(rows == height - 1, final, pltpu.roll(here, height - 1, 0))
        before = jnp.where(rows == 0, first, pltpu.roll(here, 1, 0))
        g = diffusivity(up, down, after, before, *x_sides(here))
        g_out[pl.ds(k * height, height), :] = g
        return g

    chain(g_rows, plane, depth, solved, head, tail, element)


def y_kernel(planes, height, slab, g_field, field, solved, head, tail, element):
    g_rows = lambda k: g_field[pl.ds(k, planes, stride=slab), :]
    v_rows = lambda k: field[pl.ds(k, planes, stride=slab), :]
    chain(g_rows, v_rows, height, solved, head, tail, element)


def x_kernel(first, rows, g_field, field, solved):
    width = field.shape[1]
    at = pl.ds(first, rows)
    g, right = g_field[at, :], field[at, :]
    lanes = lax.broadcasted_iota(jnp.int32, (rows, width), 1)
    link = jnp.where(lanes == width - 1, 0.0, HALF_LINK * (g + pltpu.roll(g, width - 1, 1)))
    main = 1.0 + link + pltpu.roll(link, 1, 1)
    stride = 1
    while stride < width:
        inverse = 1.0 / main
        factor = link * inverse
        back = width - stride
        ahead = link * pltpu.roll(inverse, back, 1)
        main = main - pltpu.roll(link * factor, stride, 1) - link * ahead
        right = right + pltpu.roll(factor * right, stride, 1) + ahead * pltpu.roll(right, back, 1)
        link = ahead * pltpu.roll(link, back, 1)
        stride *= 2
    solved[pl.ds(0, rows), :] = right / main


def sides(upper, own, got, last):
    pick = lambda a, b: jnp.where(upper, a, b)
    if not last:
        return [pick(g, o) for o, g in zip(own, got)], [pick(o, g) for o, g in zip(own, got)]
    zero = jnp.zeros_like(own[0])
    lower = [None, zero, pick(got[0], own[2]), None, pick(got[1], own[4])]
    higher = [pick(own[0], got[0]), zero, None, pick(own[3], got[1]), None]
    if len(own) > 5:
        lower += [None, pick(got[2], own[6])]
        higher += [pick(own[5], got[2]), None]
    return lower, higher


def join(lower, higher):
    if len(lower) == 5:
        return 1.0 / (lower[2] + higher[0]), None
    link = HALF_LINK * (lower[6] + higher[5])
    inverse = 1.0 / (1.0 + link * (lower[2] + higher[0]))
    return link * inverse, inverse


def is_upper(axis, level):
    return lax.rem(lax.div(lax.axis_index(axis), 1 << level), 2) == 1


def packed(count, rows, wide):
    return count * (rows - GHOSTS) + -(-2 * count // 8) * 8 if wide else count * rows


def put(ref, values, wide):
    rows = values[0].shape[0] - GHOSTS * wide
    for k, value in enumerate(values):
        ref[pl.ds(k * rows, rows), :] = value[:rows]
        if wide:
            ref[pl.ds(len(values) * rows + 2 * k, 2), :] = value[rows : rows + 2]


def parts(ref, rows, wide):
    if len(ref.shape) == 3:
        return [ref[k] for k in range(ref.shape[0])]
    rows -= GHOSTS * wide
    count = ref.shape[0] // rows
    values = [ref[pl.ds(k * rows, rows), :] for k in range(count)]
    if wide:
        for k in range(count):
            begin = count * rows + 2 * k
            fitting = min(begin, ref.shape[0] - 8)
            ghosts = ref[pl.ds(fitting, 8), :]
            if begin > fitting:
                ghosts = pltpu.roll(ghosts, 8 - begin + fitting, 0)
            values[k] = jnp.concatenate([values[k], ghosts], axis=0)
    return values


def merge_kernel(axis, level, last, own, got, *outs):
    upper = is_upper(axis, level)
    size, rows = own.shape[:2]
    wide = size == 5
    lower, higher = sides(upper, parts(own, rows, wide), parts(got, rows, wide), False)
    share, _ = join(lower, higher)
    gap = lower[4] - higher[3]
    first, second = share * lower[1], share * higher[1]
    merged = [
        lower[0] - first * lower[1],
        first * higher[1],
        higher[2] - second * higher[1],
        lower[3] - first * gap,
        higher[4] + second * gap,
        *([] if wide else [lower[5], higher[6]]),
    ]
    for k in range(size):
        outs[0][k] = merged[k]
    if len(outs) > 1:
        above = is_upper(axis, level + 1)
        sent = [jnp.where(above, merged[high], merged[low]) for high, low in LAST_SENT[: (size - 1) // 2]]
        put(outs[1], sent if last else merged, wide)


def unwind(axis, refs):
    rows = refs[0].shape[1]
    pairs = [parts(ref, rows, refs[0].shape[0] == 5) for ref in refs]
    zero = jnp.zeros_like(pairs[0][0])
    from_low = from_high = jump_low = jump_high = zero
    for level in range(len(pairs) // 2 - 1, -1, -1):
        upper = is_upper(axis, level)
        lower, higher = sides(upper, *pairs[2 * level : 2 * level + 2], level == len(pairs) // 2 - 1)
        share, inverse = join(lower, higher)
        gap = lower[4] - higher[3] + lower[1] * from_low - higher[1] * from_high
        flow = share * gap
        if inverse is not None:
            jump = inverse * gap
            jump_low, jump_high = jnp.where(upper, jump, jump_low), jnp.where(upper, jump_high, jump)
        from_low, from_high = jnp.where(upper, flow, from_low), jnp.where(upper, from_high, -flow)
    return from_low, from_high, jump_low, jump_high


def wide_sum_kernel(cut, height, slab, *refs):
    count = refs[-1].shape[0] // (cut * slab)
    along_x, (solved, head, tail), total = refs[:count], refs[count : count + 3], refs[-1]
    low, high, jump_low, jump_high = unwind("xy", refs[count + 3 : -1])

    def put(row, along_y):
        for k, piece in enumerate(along_x):
            at = pl.ds(k * cut * slab + row, cut, stride=slab)
            total[at, :] = piece[pl.ds(row, cut, stride=slab), :] + along_y[k * cut : (k + 1) * cut]

    for k in range(height):
        along_y = solved[k] + low * head[k] + high * tail[k]
        put(k, along_y)
        if k == 0:
            put(height, along_y + jump_low)
        if k == height - 1:
            put(height + 1, along_y - jump_high)


def sum_kernel(cut, height, *refs):
    count = refs[-1].shape[0] // (cut * height)
    along_x, (solved, head, tail), total = refs[:count], refs[count : count + 3], refs[-1]
    low, high, _, _ = unwind("xy", refs[count + 3 : -1])
    for row in range(height):
        along_y = solved[row] + low * head[row] + high * tail[row]
        for k, piece in enumerate(along_x):
            at = pl.ds(k * cut * height + row, cut, stride=height)
            total[at, :] = piece[pl.ds(row, cut, stride=height), :] + along_y[k * cut : (k + 1) * cut]


def step_kernel(depth, height, total, solved, head, tail, w_low, w_high, *refs):
    field, near, far, below, above = refs[-5:]
    slab = height + GHOSTS
    low, high, _, _ = unwind("gz", refs[:-5])
    for k in range(depth):
        along_z = solved[k] + low * head[k] + high * tail[k]
        value = (total[pl.ds(k * slab, slab), :] + along_z) * THIRD
        field[pl.ds(k * height, height), :] = value[:height]
        near[pl.ds(k, 1), :] = value[height : height + 1]
        far[pl.ds(k, 1), :] = value[height + 1 : height + 2]
        if k == 0:
            along_z = along_z + low / w_low[...]
            below[...] = (total[pl.ds(depth * slab, height), :] + along_z[:height]) * THIRD
        if k == depth - 1:
            along_z = solved[k] + low * head[k] + high * tail[k] + high / w_high[...]
            above[...] = (total[pl.ds((depth + 1) * slab, height), :] + along_z[:height]) * THIRD


def last_kernel(depth, height, total, solved, head, tail, slots, *refs):
    chunks = refs[-len(CHUNKS) :]
    low, high, _, _ = unwind("gz", refs[: -len(CHUNKS)])
    planes = BLOCK_ROWS // height
    for k in range(depth):
        value = (total[pl.ds(k * height, height), :] + (solved[k] + low * head[k] + high * tail[k])) * THIRD
        block, row, chunk = k // planes, (k % planes) * height, 0
        while row >= CHUNKS[chunk]:
            row, chunk = row - CHUNKS[chunk], chunk + 1
        chunks[chunk][pl.ds(block * CHUNKS[chunk] + row, height), :] = value
    chunks[0][pl.ds(depth // planes * CHUNKS[0], slots.shape[0]), :] = slots[...]


def pack_kernel(ways, number, sizes, *refs):
    pieces, outs = refs[: len(sizes)], refs[-ways:]
    slots, begin = (refs[0], number * sizes[0]) if len(refs) == len(sizes) + ways else (refs[len(sizes)], 0)
    me = lax.axis_index("gz")
    place = lax.rem(me, ways)
    placed = [jnp.max(slots[pl.ds(begin + block, 1), :]).astype(jnp.int32) for block in range(number)]
    for out in outs:
        out[...] = jnp.zeros_like(out)
    for block, slot in enumerate(placed):
        rank, target = lax.rem(slot, MOST), lax.div(slot, MOST) - (me - place)
        for way, out in enumerate(outs):

            @pl.when(target == lax.bitwise_xor(place, way))
            def _():
                row = 0
                for size, piece in zip(sizes, pieces):
                    out[rank, pl.ds(row, size), :] = piece[pl.ds(block * size, size), :]
                    row += size


def pack(ways, number, pieces, sizes, slots):
    shape = (MOST, sum(sizes), pieces[0].shape[1])
    return call(functools.partial(pack_kernel, ways, number, sizes), [shape] * ways, [*pieces, *slots])


def place_kernel(plan, kept, fresh, *refs):
    count = len(plan) + len(kept)
    outs, sems = refs[count + (not fresh) : -1], refs[-1]
    me = lax.axis_index("gz")
    moves, row = [], 0
    for k, (way, begin) in enumerate(plan):
        source = lax.bitwise_xor(me, way)
        rows = refs[k].shape[1]
        moves.append((refs[k], outs[0].at[pl.ds(source * MOST, MOST), pl.ds(begin, rows), :]))
    for size, ref in zip(kept, refs[len(plan) : count]):
        for block in range(outs[1].shape[0]):
            moves.append((ref.at[pl.ds(block * size, size), :], outs[1].at[block, pl.ds(row, size), :]))
        row += size
    copies = [pltpu.make_async_copy(*move, sems.at[k]) for k, move in enumerate(moves)]
    for copy in copies:
        copy.start()
    for copy in copies:
        copy.wait()


def place(arrays, plan, incoming, shapes, kept=()):
    count = len(arrays) + len(kept)
    copies = len(arrays) + len(kept) * (shapes[1][0] if kept else 0)
    extra = [] if incoming is None else [incoming]
    return pl.pallas_call(
        functools.partial(place_kernel, plan, CHUNKS if kept else (), not extra),
        out_shape=[jax.ShapeDtypeStruct(shape, jnp.float32) for shape in shapes],
        in_specs=[pl.BlockSpec(memory_space=VMEM)] * count + [pl.BlockSpec(memory_space=pl.ANY)] * len(extra),
        out_specs=[pl.BlockSpec(memory_space=pl.ANY)] * len(shapes),
        scratch_shapes=[pltpu.SemaphoreType.DMA((copies,))],
        input_output_aliases={count: 0} if extra else {},
        compiler_params=pltpu.CompilerParams(vmem_limit_bytes=VMEM_LIMIT),
    )(*arrays, *kept, *extra)


def swap(values, axis, stride):
    count = lax.axis_size(axis)
    return lax.ppermute(values, axis, [(i, i ^ stride) for i in range(count)])


def near(first, axis):
    return swap(first, axis, 1)


def far(second, axis):
    count = lax.axis_size(axis)
    if axis == "xy":
        other = [(i, (i + 1) % count) for i in range(1, count, 2)]
        return lax.ppermute(second, axis, other + [(j, i) for i, j in other])
    beside = lax.axis_size("xy")
    pairs = []
    for i in range(count):
        end = i in (0, count - 1)
        j = i if end else i + 1 if i % 2 else i - 1
        pairs += [(i * beside + c, j * beside + (c ^ 1 if end else c)) for c in range(beside)]
    return lax.ppermute(second, (axis, "xy"), pairs)


def neighbours(first, second, axis):
    got = far(second, axis)
    return near(first, axis), got


def merge(element, got, axis, level, after=()):
    size, rows, width = element.shape
    last, wide = 4 << level >= lax.axis_size(axis), size == 5
    count = (size - 1) // 2 if last else size
    outs = [element.shape] + [(packed(count, rows, wide), width)] * (last or wide)
    merged = call(functools.partial(merge_kernel, axis, level, last), outs, [element, got], after=after)
    return merged[0], merged[-1]


def route(chunks, slots, number):
    count, width = lax.axis_size("gz"), chunks[0].shape[1]
    ways = count // 2
    order = range(ways - 1, 0, -1)
    crossed = []
    for chunk in chunks:
        crossed.append(swap(chunk, "gz", ways))
    straight = pack(ways, number, chunks, CHUNKS, [slots])
    arrays = [straight[0]]
    for way in order:
        arrays.append(swap(straight[way], "gz", way))
    shapes = [(count * MOST, BLOCK_ROWS, width), (number, BLOCK_ROWS, width)]
    plan = [(way, 0) for way in (0, *order)]
    incoming, field = place(arrays, plan, None, shapes, chunks)
    row = 0
    for k, size in enumerate(CHUNKS):
        others = [] if k == 0 else [lax.slice_in_dim(crossed[0], number * CHUNKS[0], None, axis=0)]
        passed = pack(ways, number, crossed[k : k + 1], (size,), others)
        arrays = [passed[0]]
        for way in order:
            arrays.append(swap(passed[way], "gz", way))
        plan = [(way ^ ways, row) for way in (0, *order)]
        (incoming,) = place(arrays, plan, incoming, shapes[:1])
        row += size
    return field, incoming


def lines(field, g_field, z_element, z_sent, planes, height, slab, used, sum_body):
    width = field.shape[1]
    part = functools.partial
    z_rounds, y_rounds = (lax.axis_size(axis).bit_length() - 1 for axis in ("gz", "xy"))
    y_shape = (height, planes, width)
    *y_pieces, y_element = call(
        part(y_kernel, planes, height, slab),
        [y_shape, y_shape, y_shape, (7, planes, width)],
        [g_field, field],
        after=[z_element],
    )
    y_start, y_sent, y_pairs = y_element, y_element, []
    for level in range(y_rounds):
        y_pairs += [y_element, swap(y_sent, "xy", 1 << level)]
        if level + 1 < y_rounds:
            y_element, y_sent = merge(*y_pairs[-2:], "xy", level)
    cut, along_x = 8, {}
    order = [0, 2, 1] if planes > 2 * cut else [0, 1]

    def x_part(after):
        turn = len(along_x)
        k = order[turn]
        rows = min(cut, used - k * cut) * slab
        (along_x[k],) = call(part(x_kernel, k * cut * slab, rows), [(cut * slab, width)], [g_field, field], after=after)

    z_pairs = []
    for level in range(z_rounds):
        z_pairs += [z_element, swap(z_sent, "gz", 1 << level)]
        behind = []
        if level == 0:
            x_part([y_start])
            behind = [along_x[order[0]], y_element]
        if level == 1:
            x_part([z_element])
            behind = [along_x[order[1]]]
        if level == 2:
            while len(along_x) < len(order):
                x_part([z_element])
            (total,) = call(
                part(sum_body, cut), [(planes * slab, width)], [*(along_x[k] for k in range(len(order))), *y_pieces, *y_pairs]
            )
        if level + 1 < z_rounds:
            z_element, z_sent = merge(*z_pairs[-2:], "gz", level, behind)
    return total, z_pairs


def on_device(volume, owners):
    depth, height, width = volume.shape
    slab = height + GHOSTS
    planes = -(-(depth + 4) // 8) * 8
    blocks = owners.shape[1]
    part = functools.partial
    flat, plane, side = (depth * height, width), (height, width), (depth, width)

    field = volume.reshape(flat)
    edges = call(part(edge_kernel, depth, height), [(2 * depth, width)] * 2, [field])
    y_sides = neighbours(*edges, "xy")
    slabs, *edges = call(
        part(slab_kernel, depth, height), [(depth * slab, width)] + [(2 * slab, width)] * 2, [field, *y_sides]
    )
    z_sides = neighbours(*edges, "gz")
    slots = slots_of(owners, width, edges[0])
    field, g_field, *z_pieces, z_element, w_low, w_high, z_sent = call(
        part(wide_kernel, depth, height),
        [(planes * slab, width)] * 2 + [(depth, slab, width)] * 3 + [(5, slab, width)] + [(slab, width)] * 2 + [(packed(5, slab, True), width)],
        [slabs, *z_sides],
        after=[slots],
    )
    total, z_pairs = lines(
        field, g_field, z_element, z_sent, planes, height, slab, depth + 2, lambda cut, *refs: wide_sum_kernel(cut, height, slab, *refs)
    )
    field, *around = call(
        part(step_kernel, depth, height), [flat, side, side, plane, plane], [total, *z_pieces, w_low, w_high, *z_pairs]
    )
    g_field, *z_pieces, z_element = call(
        part(z_kernel, depth, height), [flat] + [(depth, height, width)] * 3 + [(7, height, width)], [field, *around]
    )
    total, z_pairs = lines(
        field, g_field, z_element, z_element, depth, height, height, depth, lambda cut, *refs: sum_kernel(cut, height, *refs)
    )
    rows = slots.shape[0]
    chunks = call(
        part(last_kernel, depth, height),
        [(blocks * size + rows * (k == 0), width) for k, size in enumerate(CHUNKS)],
        [total, *z_pieces, slots, *z_pairs],
    )
    field, incoming = route(chunks, slots, blocks)
    return field.reshape(volume.shape), incoming[None]


def solution(mesh):
    in_specs = (P("gz", "xy", None), P("xy", "gz", None))
    out_specs = (P("gz", "xy", None), P("xy", "gz", None, None))

    return jax.shard_map(on_device, mesh=mesh, in_specs=in_specs, out_specs=out_specs, check_vma=False)
```

```python
import functools

import jax
import jax.numpy as jnp
from jax import lax
from jax.experimental import pallas as pl
from jax.experimental.pallas import tpu as pltpu
from jax.sharding import PartitionSpec as P


MOST = 2
CHUNKS = (128,)
BLOCK_ROWS = 128
TIME_STEP = 30.0
CONTRAST = 4.0
HALF_LINK = 1.5 * TIME_STEP
THIRD = 1.0 / 3.0
GHOSTS = 8
LAST_SENT = ((0, 2), (3, 4), (5, 6))
VMEM_LIMIT = 16 * 1024 * 1024
VMEM = pltpu.VMEM


def call(body, outs, ins, after=()):
    count = len(ins)
    specs = [pl.BlockSpec(memory_space=VMEM)] * count + [pl.BlockSpec(memory_space=pl.ANY)] * len(after)
    return pl.pallas_call(
        lambda *refs: body(*refs[:count], *refs[count + len(after) :]),
        out_shape=[jax.ShapeDtypeStruct(shape, jnp.float32) for shape in outs],
        in_specs=specs,
        out_specs=[pl.BlockSpec(memory_space=VMEM)] * len(outs),
        compiler_params=pltpu.CompilerParams(vmem_limit_bytes=VMEM_LIMIT),
    )(*ins, *after)


def edge_kernel(depth, height, field, y_first, y_second):
    y_odd = lax.rem(lax.axis_index("xy"), 2) == 1
    for k in range(2):
        near = field[pl.ds(k, depth, stride=height), :]
        far = field[pl.ds(height - 1 - k, depth, stride=height), :]
        y_first[pl.ds(k * depth, depth), :] = jnp.where(y_odd, near, far)
        y_second[pl.ds(k * depth, depth), :] = jnp.where(y_odd, far, near)


def slab_kernel(depth, height, field, y_first, y_second, slabs, z_first, z_second):
    slab = height + GHOSTS
    y_odd = lax.rem(lax.axis_index("xy"), 2) == 1
    for k in range(depth):
        slabs[pl.ds(k * slab, height), :] = field[pl.ds(k * height, height), :]
    for k in range(2):
        one, two = y_first[pl.ds(k * depth, depth), :], y_second[pl.ds(k * depth, depth), :]
        slabs[pl.ds(height + 2 * k, depth, stride=slab), :] = jnp.where(y_odd, one, two)
        slabs[pl.ds(height + 2 * k + 1, depth, stride=slab), :] = jnp.where(y_odd, two, one)
    for k in range(4, GHOSTS):
        slabs[pl.ds(height + k, depth, stride=slab), :] = jnp.zeros((depth, field.shape[1]), field.dtype)
    z_odd = lax.rem(lax.axis_index("gz"), 2) == 1
    for k in range(2):
        low, high = slabs[pl.ds(k * slab, slab), :], slabs[pl.ds((depth - 1 - k) * slab, slab), :]
        z_first[pl.ds(k * slab, slab), :] = jnp.where(z_odd, low, high)
        z_second[pl.ds(k * slab, slab), :] = jnp.where(z_odd, high, low)


def slot_kernel(given, first, slots, owners, sem):
    copy = pltpu.make_async_copy(given, owners, sem)
    copy.start()
    slots[...] = jnp.zeros_like(slots)
    copy.wait()
    for block in range(owners.shape[1]):
        rank = jnp.int32(0)
        for other in range(block):
            rank = rank + (owners[0, other] == owners[0, block]).astype(jnp.int32)
        slot = owners[0, block] * MOST + rank
        slots[pl.ds(block, 1), :] = jnp.full((1, slots.shape[1]), slot.astype(jnp.float32))


def slots_of(owners, width, after):
    blocks = owners.shape[1]
    return pl.pallas_call(
        slot_kernel,
        out_shape=jax.ShapeDtypeStruct((-(-blocks // 8) * 8, width), jnp.float32),
        in_specs=[pl.BlockSpec(memory_space=pl.ANY)] * 2,
        out_specs=pl.BlockSpec(memory_space=VMEM),
        scratch_shapes=[pltpu.SMEM((1, blocks), jnp.int32), pltpu.SemaphoreType.DMA],
        compiler_params=pltpu.CompilerParams(vmem_limit_bytes=VMEM_LIMIT),
        name="slots",
    )(owners.reshape(1, blocks), after)


def chain(g_rows, v_rows, count, solved, head, tail, element):
    g_head = g_prev = g_rows(0)
    pivot = jnp.ones_like(g_prev)
    right = v_rows(0)
    unit = pivot
    for k in range(count - 1):
        g_next = g_rows(k + 1)
        link = HALF_LINK * (g_prev + g_next)
        inverse = 1.0 / (pivot + link)
        ratio = link * inverse
        solved[k] = right * inverse
        head[k] = unit * inverse
        tail[k] = ratio
        pivot = 1.0 + ratio * pivot
        right = v_rows(k + 1) + ratio * right
        unit = ratio * unit
        g_prev = g_next
    inverse = 1.0 / pivot
    value, from_head, from_tail = right * inverse, unit * inverse, inverse
    solved[count - 1] = value
    head[count - 1] = from_head
    tail[count - 1] = from_tail
    element[2] = from_tail
    element[4] = value
    if element.shape[0] > 5:
        element[5] = g_head
        element[6] = g_prev
    for k in range(count - 2, -1, -1):
        ratio = tail[k]
        value = solved[k] + ratio * value
        from_head = head[k] + ratio * from_head
        from_tail = ratio * from_tail
        solved[k] = value
        head[k] = from_head
        tail[k] = from_tail
    element[0] = from_head
    element[1] = from_tail
    element[3] = value


def diffusivity(up, down, after, before, right, left):
    squares = ((up - down) * 0.5) * ((up - down) * 0.5)
    slope = (after - before) * 0.5
    squares = squares + slope * slope
    slope = (right - left) * 0.5
    squares = squares + slope * slope
    return 1.0 / (1.0 + squares * (1.0 / CONTRAST))


def x_sides(here):
    width = here.shape[1]
    lanes = lax.broadcasted_iota(jnp.int32, here.shape, 1)
    right = jnp.where(lanes == width - 1, here, pltpu.roll(here, width - 1, 1))
    return right, jnp.where(lanes == 0, here, pltpu.roll(here, 1, 1))


def ends(axis):
    index = lax.axis_index(axis)
    return index == 0, index == lax.axis_size(axis) - 1


def wide_kernel(depth, height, slabs, z_first, z_second, field, g_out, solved, head, tail, element, w_low, w_high, sent):
    slab = height + GHOSTS
    width = slabs.shape[1]
    z_odd = lax.rem(lax.axis_index("gz"), 2) == 1
    z_begin, z_end = ends("gz")
    y_begin, y_end = ends("xy")
    rows = lax.broadcasted_iota(jnp.int32, (slab, width), 0)
    own = depth * slab
    field[pl.ds(0, own), :] = slabs[...]
    for k in range(2):
        one, two = z_first[pl.ds(k * slab, slab), :], z_second[pl.ds(k * slab, slab), :]
        field[pl.ds(own + 2 * k * slab, slab), :] = jnp.where(z_odd, one, two)
        field[pl.ds(own + (2 * k + 1) * slab, slab), :] = jnp.where(z_odd, two, one)
    spare = field.shape[0] - own - 4 * slab
    field[pl.ds(own + 4 * slab, spare), :] = jnp.zeros((spare, width), field.dtype)
    g_out[pl.ds(own + 2 * slab, spare + 2 * slab), :] = jnp.ones((spare + 2 * slab, width), field.dtype)

    def begin(k):
        if k < 0:
            return own + (2 if k < -1 else 0) * slab
        return own + (1 + 2 * (k - depth)) * slab if k >= depth else k * slab

    plane = lambda k: field[pl.ds(begin(k), slab), :]

    def g_rows(k):
        here, up, down = plane(k), plane(k + 1), plane(k - 1)
        if k == 0:
            down = jnp.where(z_begin, here, down)
        if k == depth - 1:
            up = jnp.where(z_end, here, up)
        row = lambda r: field[pl.ds(begin(k) + r, 1), :]
        first, final = row(0), row(height - 1)
        after = jnp.where(rows == height - 1, jnp.where(y_end, final, row(height + 1)), pltpu.roll(here, slab - 1, 0))
        after = jnp.where(rows == height, first, jnp.where(rows == height + 1, row(height + 3), after))
        before = jnp.where(rows == 0, jnp.where(y_begin, first, row(height)), pltpu.roll(here, 1, 0))
        before = jnp.where(rows == height, row(height + 2), jnp.where(rows == height + 1, final, before))
        g = diffusivity(up, down, after, before, *x_sides(here))
        g_out[pl.ds(begin(k), slab), :] = g
        return g

    chain(g_rows, plane, depth, solved, head, tail, element)
    g_own = lambda k: g_out[pl.ds(k * slab, slab), :]
    w_low[...] = HALF_LINK * (g_own(0) + g_rows(-1))
    link = HALF_LINK * (g_own(depth - 1) + g_rows(depth))
    w_high[...] = link
    element[2] = element[2] + 1.0 / link
    put(sent, [element[k] for k in range(5)], True)


def z_kernel(depth, height, field, near, far, low, high, g_out, solved, head, tail, element):
    plane = lambda k: field[pl.ds(k * height, height), :]
    z_begin, z_end = ends("gz")
    y_begin, y_end = ends("xy")
    below = jnp.where(z_begin, plane(0), low[...])
    above = jnp.where(z_end, plane(depth - 1), high[...])
    rows = lax.broadcasted_iota(jnp.int32, (height, field.shape[1]), 0)

    def g_rows(k):
        here = plane(k)
        up, down = plane(k + 1) if k < depth - 1 else above, plane(k - 1) if k else below
        first = jnp.where(y_begin, here[:1], near[pl.ds(k, 1), :])
        final = jnp.where(y_end, here[height - 1 :], far[pl.ds(k, 1), :])
        after = jnp.where(rows == height - 1, final, pltpu.roll(here, height - 1, 0))
        before = jnp.where(rows == 0, first, pltpu.roll(here, 1, 0))
        g = diffusivity(up, down, after, before, *x_sides(here))
        g_out[pl.ds(k * height, height), :] = g
        return g

    chain(g_rows, plane, depth, solved, head, tail, element)


def y_kernel(planes, height, slab, g_field, field, solved, head, tail, element):
    g_rows = lambda k: g_field[pl.ds(k, planes, stride=slab), :]
    v_rows = lambda k: field[pl.ds(k, planes, stride=slab), :]
    chain(g_rows, v_rows, height, solved, head, tail, element)


def x_kernel(first, rows, g_field, field, solved):
    width = field.shape[1]
    at = pl.ds(first, rows)
    g, right = g_field[at, :], field[at, :]
    lanes = lax.broadcasted_iota(jnp.int32, (rows, width), 1)
    link = jnp.where(lanes == width - 1, 0.0, HALF_LINK * (g + pltpu.roll(g, width - 1, 1)))
    main = 1.0 + link + pltpu.roll(link, 1, 1)
    stride = 1
    while stride < width:
        inverse = 1.0 / main
        factor = link * inverse
        back = width - stride
        ahead = link * pltpu.roll(inverse, back, 1)
        main = main - pltpu.roll(link * factor, stride, 1) - link * ahead
        right = right + pltpu.roll(factor * right, stride, 1) + ahead * pltpu.roll(right, back, 1)
        link = ahead * pltpu.roll(link, back, 1)
        stride *= 2
    solved[pl.ds(0, rows), :] = right / main


def sides(upper, own, got, last):
    pick = lambda a, b: jnp.where(upper, a, b)
    if not last:
        return [pick(g, o) for o, g in zip(own, got)], [pick(o, g) for o, g in zip(own, got)]
    zero = jnp.zeros_like(own[0])
    lower = [None, zero, pick(got[0], own[2]), None, pick(got[1], own[4])]
    higher = [pick(own[0], got[0]), zero, None, pick(own[3], got[1]), None]
    if len(own) > 5:
        lower += [None, pick(got[2], own[6])]
        higher += [pick(own[5], got[2]), None]
    return lower, higher


def join(lower, higher):
    if len(lower) == 5:
        return 1.0 / (lower[2] + higher[0]), None
    link = HALF_LINK * (lower[6] + higher[5])
    inverse = 1.0 / (1.0 + link * (lower[2] + higher[0]))
    return link * inverse, inverse


def is_upper(axis, level):
    return lax.rem(lax.div(lax.axis_index(axis), 1 << level), 2) == 1


def packed(count, rows, wide):
    return count * (rows - GHOSTS) + -(-2 * count // 8) * 8 if wide else count * rows


def put(ref, values, wide):
    rows = values[0].shape[0] - GHOSTS * wide
    for k, value in enumerate(values):
        ref[pl.ds(k * rows, rows), :] = value[:rows]
        if wide:
            ref[pl.ds(len(values) * rows + 2 * k, 2), :] = value[rows : rows + 2]


def parts(ref, rows, wide):
    if len(ref.shape) == 3:
        return [ref[k] for k in range(ref.shape[0])]
    rows -= GHOSTS * wide
    count = ref.shape[0] // rows
    values = [ref[pl.ds(k * rows, rows), :] for k in range(count)]
    if wide:
        for k in range(count):
            begin = count * rows + 2 * k
            fitting = min(begin, ref.shape[0] - 8)
            ghosts = ref[pl.ds(fitting, 8), :]
            if begin > fitting:
                ghosts = pltpu.roll(ghosts, 8 - begin + fitting, 0)
            values[k] = jnp.concatenate([values[k], ghosts], axis=0)
    return values


def merge_kernel(axis, level, last, own, got, *outs):
    upper = is_upper(axis, level)
    size, rows = own.shape[:2]
    wide = size == 5
    lower, higher = sides(upper, parts(own, rows, wide), parts(got, rows, wide), False)
    share, _ = join(lower, higher)
    gap = lower[4] - higher[3]
    first, second = share * lower[1], share * higher[1]
    merged = [
        lower[0] - first * lower[1],
        first * higher[1],
        higher[2] - second * higher[1],
        lower[3] - first * gap,
        higher[4] + second * gap,
        *([] if wide else [lower[5], higher[6]]),
    ]
    for k in range(size):
        outs[0][k] = merged[k]
    if len(outs) > 1:
        above = is_upper(axis, level + 1)
        sent = [jnp.where(above, merged[high], merged[low]) for high, low in LAST_SENT[: (size - 1) // 2]]
        put(outs[1], sent if last else merged, wide)


def unwind(axis, refs):
    rows = refs[0].shape[1]
    pairs = [parts(ref, rows, refs[0].shape[0] == 5) for ref in refs]
    zero = jnp.zeros_like(pairs[0][0])
    from_low = from_high = jump_low = jump_high = zero
    for level in range(len(pairs) // 2 - 1, -1, -1):
        upper = is_upper(axis, level)
        lower, higher = sides(upper, *pairs[2 * level : 2 * level + 2], level == len(pairs) // 2 - 1)
        share, inverse = join(lower, higher)
        gap = lower[4] - higher[3] + lower[1] * from_low - higher[1] * from_high
        flow = share * gap
        if inverse is not None:
            jump = inverse * gap
            jump_low, jump_high = jnp.where(upper, jump, jump_low), jnp.where(upper, jump_high, jump)
        from_low, from_high = jnp.where(upper, flow, from_low), jnp.where(upper, from_high, -flow)
    return from_low, from_high, jump_low, jump_high


def wide_sum_kernel(cut, height, slab, *refs):
    count = refs[-1].shape[0] // (cut * slab)
    along_x, (solved, head, tail), total = refs[:count], refs[count : count + 3], refs[-1]
    low, high, jump_low, jump_high = unwind("xy", refs[count + 3 : -1])

    def put(row, along_y):
        for k, piece in enumerate(along_x):
            at = pl.ds(k * cut * slab + row, cut, stride=slab)
            total[at, :] = piece[pl.ds(row, cut, stride=slab), :] + along_y[k * cut : (k + 1) * cut]

    for k in range(height):
        along_y = solved[k] + low * head[k] + high * tail[k]
        put(k, along_y)
        if k == 0:
            put(height, along_y + jump_low)
        if k == height - 1:
            put(height + 1, along_y - jump_high)


def sum_kernel(cut, height, *refs):
    count = refs[-1].shape[0] // (cut * height)
    along_x, (solved, head, tail), total = refs[:count], refs[count : count + 3], refs[-1]
    low, high, _, _ = unwind("xy", refs[count + 3 : -1])
    for row in range(height):
        along_y = solved[row] + low * head[row] + high * tail[row]
        for k, piece in enumerate(along_x):
            at = pl.ds(k * cut * height + row, cut, stride=height)
            total[at, :] = piece[pl.ds(row, cut, stride=height), :] + along_y[k * cut : (k + 1) * cut]


def step_kernel(depth, height, total, solved, head, tail, w_low, w_high, *refs):
    field, near, far, below, above = refs[-5:]
    slab = height + GHOSTS
    low, high, _, _ = unwind("gz", refs[:-5])
    for k in range(depth):
        along_z = solved[k] + low * head[k] + high * tail[k]
        value = (total[pl.ds(k * slab, slab), :] + along_z) * THIRD
        field[pl.ds(k * height, height), :] = value[:height]
        near[pl.ds(k, 1), :] = value[height : height + 1]
        far[pl.ds(k, 1), :] = value[height + 1 : height + 2]
        if k == 0:
            along_z = along_z + low / w_low[...]
            below[...] = (total[pl.ds(depth * slab, height), :] + along_z[:height]) * THIRD
        if k == depth - 1:
            along_z = solved[k] + low * head[k] + high * tail[k] + high / w_high[...]
            above[...] = (total[pl.ds((depth + 1) * slab, height), :] + along_z[:height]) * THIRD


def last_kernel(depth, height, total, solved, head, tail, slots, *refs):
    chunks = refs[-len(CHUNKS) :]
    low, high, _, _ = unwind("gz", refs[: -len(CHUNKS)])
    planes = BLOCK_ROWS // height
    for k in range(depth):
        value = (total[pl.ds(k * height, height), :] + (solved[k] + low * head[k] + high * tail[k])) * THIRD
        block, row, chunk = k // planes, (k % planes) * height, 0
        while row >= CHUNKS[chunk]:
            row, chunk = row - CHUNKS[chunk], chunk + 1
        chunks[chunk][pl.ds(block * CHUNKS[chunk] + row, height), :] = value
    chunks[0][pl.ds(depth // planes * CHUNKS[0], slots.shape[0]), :] = slots[...]


def pack_kernel(ways, number, sizes, *refs):
    pieces, outs = refs[: len(sizes)], refs[-ways:]
    slots, begin = (refs[0], number * sizes[0]) if len(refs) == len(sizes) + ways else (refs[len(sizes)], 0)
    me = lax.axis_index("gz")
    place = lax.rem(me, ways)
    placed = [jnp.max(slots[pl.ds(begin + block, 1), :]).astype(jnp.int32) for block in range(number)]
    for out in outs:
        out[...] = jnp.zeros_like(out)
    for block, slot in enumerate(placed):
        rank, target = lax.rem(slot, MOST), lax.div(slot, MOST) - (me - place)
        for way, out in enumerate(outs):

            @pl.when(target == lax.bitwise_xor(place, way))
            def _():
                row = 0
                for size, piece in zip(sizes, pieces):
                    out[rank, pl.ds(row, size), :] = piece[pl.ds(block * size, size), :]
                    row += size


def pack(ways, number, pieces, sizes, slots):
    shape = (MOST, sum(sizes), pieces[0].shape[1])
    return call(functools.partial(pack_kernel, ways, number, sizes), [shape] * ways, [*pieces, *slots])


def place_kernel(plan, kept, fresh, *refs):
    count = len(plan) + len(kept)
    outs, sems = refs[count + (not fresh) : -1], refs[-1]
    me = lax.axis_index("gz")
    moves, row = [], 0
    for k, (way, begin) in enumerate(plan):
        source = lax.bitwise_xor(me, way)
        rows = refs[k].shape[1]
        moves.append((refs[k], outs[0].at[pl.ds(source * MOST, MOST), pl.ds(begin, rows), :]))
    for size, ref in zip(kept, refs[len(plan) : count]):
        for block in range(outs[1].shape[0]):
            moves.append((ref.at[pl.ds(block * size, size), :], outs[1].at[block, pl.ds(row, size), :]))
        row += size
    copies = [pltpu.make_async_copy(*move, sems.at[k]) for k, move in enumerate(moves)]
    for copy in copies:
        copy.start()
    for copy in copies:
        copy.wait()


def place(arrays, plan, incoming, shapes, kept=()):
    count = len(arrays) + len(kept)
    copies = len(arrays) + len(kept) * (shapes[1][0] if kept else 0)
    extra = [] if incoming is None else [incoming]
    return pl.pallas_call(
        functools.partial(place_kernel, plan, CHUNKS if kept else (), not extra),
        out_shape=[jax.ShapeDtypeStruct(shape, jnp.float32) for shape in shapes],
        in_specs=[pl.BlockSpec(memory_space=VMEM)] * count + [pl.BlockSpec(memory_space=pl.ANY)] * len(extra),
        out_specs=[pl.BlockSpec(memory_space=pl.ANY)] * len(shapes),
        scratch_shapes=[pltpu.SemaphoreType.DMA((copies,))],
        input_output_aliases={count: 0} if extra else {},
        compiler_params=pltpu.CompilerParams(vmem_limit_bytes=VMEM_LIMIT),
    )(*arrays, *kept, *extra)


def swap(values, axis, stride):
    count = lax.axis_size(axis)
    return lax.ppermute(values, axis, [(i, i ^ stride) for i in range(count)])


def near(first, axis):
    return swap(first, axis, 1)


def far(second, axis):
    count = lax.axis_size(axis)
    if axis == "xy":
        other = [(i, (i + 1) % count) for i in range(1, count, 2)]
        return lax.ppermute(second, axis, other + [(j, i) for i, j in other])
    beside = lax.axis_size("xy")
    pairs = []
    for i in range(count):
        end = i in (0, count - 1)
        j = i if end else i + 1 if i % 2 else i - 1
        pairs += [(i * beside + c, j * beside + (c ^ 1 if end else c)) for c in range(beside)]
    return lax.ppermute(second, (axis, "xy"), pairs)


def neighbours(first, second, axis):
    got = far(second, axis)
    return near(first, axis), got


def merge(element, got, axis, level, after=()):
    size, rows, width = element.shape
    last, wide = 4 << level >= lax.axis_size(axis), size == 5
    count = (size - 1) // 2 if last else size
    outs = [element.shape] + [(packed(count, rows, wide), width)] * (last or wide)
    merged = call(functools.partial(merge_kernel, axis, level, last), outs, [element, got], after=after)
    return merged[0], merged[-1]


def route(chunks, slots, number):
    count, width = lax.axis_size("gz"), chunks[0].shape[1]
    ways = count // 2
    order = range(ways - 1, 0, -1)
    crossed = []
    for chunk in chunks:
        crossed.append(swap(chunk, "gz", ways))
    straight = pack(ways, number, chunks, CHUNKS, [slots])
    arrays = [straight[0]]
    for way in order:
        arrays.append(swap(straight[way], "gz", way))
    shapes = [(count * MOST, BLOCK_ROWS, width), (number, BLOCK_ROWS, width)]
    plan = [(way, 0) for way in (0, *order)]
    incoming, field = place(arrays, plan, None, shapes, chunks)
    row = 0
    for k, size in enumerate(CHUNKS):
        others = [] if k == 0 else [lax.slice_in_dim(crossed[0], number * CHUNKS[0], None, axis=0)]
        passed = pack(ways, number, crossed[k : k + 1], (size,), others)
        arrays = [passed[0]]
        for way in order:
            arrays.append(swap(passed[way], "gz", way))
        plan = [(way ^ ways, row) for way in (0, *order)]
        (incoming,) = place(arrays, plan, incoming, shapes[:1])
        row += size
    return field, incoming


def lines(step, owners, field, g_field, z_element, z_sent, planes, height, slab, used, sum_body):
    width = field.shape[1]
    part = functools.partial
    z_rounds, y_rounds = (lax.axis_size(axis).bit_length() - 1 for axis in ("gz", "xy"))
    y_shape = (height, planes, width)
    *y_pieces, y_element = call(
        part(y_kernel, planes, height, slab),
        [y_shape, y_shape, y_shape, (7, planes, width)],
        [g_field, field],
        after=[z_element],
    )
    y_start, y_sent, y_pairs = y_element, y_element, []
    for level in range(y_rounds):
        y_pairs += [y_element, swap(y_sent, "xy", 1 << level)]
        if level + 1 < y_rounds:
            y_element, y_sent = merge(*y_pairs[-2:], "xy", level)
    cut, along_x = 8, {}
    order = [0, 2, 1] if planes > 2 * cut else [0, 1]

    def x_part(after):
        turn = len(along_x)
        k = order[turn]
        rows = min(cut, used - k * cut) * slab
        (along_x[k],) = call(part(x_kernel, k * cut * slab, rows), [(cut * slab, width)], [g_field, field], after=after)

    z_pairs, slots = [], None
    for level in range(z_rounds):
        z_pairs += [z_element, swap(z_sent, "gz", 1 << level)]
        behind = []
        if level == 0:
            x_part([y_start])
            behind = [along_x[order[0]], y_element]
        if level == 1:
            x_part([z_element])
            behind = [along_x[order[1]]]
            if step == 0:
                slots = slots_of(owners, width, z_element)
                behind.append(slots)
        if level == 2:
            while len(along_x) < len(order):
                x_part([z_element])
            (total,) = call(
                part(sum_body, cut), [(planes * slab, width)], [*(along_x[k] for k in range(len(order))), *y_pieces, *y_pairs]
            )
        if level + 1 < z_rounds:
            z_element, z_sent = merge(*z_pairs[-2:], "gz", level, behind)
    return total, z_pairs, slots


def on_device(volume, owners):
    depth, height, width = volume.shape
    slab = height + GHOSTS
    planes = -(-(depth + 4) // 8) * 8
    blocks = owners.shape[1]
    part = functools.partial
    flat, plane, side = (depth * height, width), (height, width), (depth, width)

    field = volume.reshape(flat)
    edges = call(part(edge_kernel, depth, height), [(2 * depth, width)] * 2, [field])
    y_sides = neighbours(*edges, "xy")
    slabs, *edges = call(
        part(slab_kernel, depth, height), [(depth * slab, width)] + [(2 * slab, width)] * 2, [field, *y_sides]
    )
    z_sides = neighbours(*edges, "gz")
    field, g_field, *z_pieces, z_element, w_low, w_high, z_sent = call(
        part(wide_kernel, depth, height),
        [(planes * slab, width)] * 2 + [(depth, slab, width)] * 3 + [(5, slab, width)] + [(slab, width)] * 2 + [(packed(5, slab, True), width)],
        [slabs, *z_sides],
    )
    total, z_pairs, slots = lines(
        0, owners, field, g_field, z_element, z_sent, planes, height, slab, depth + 2, lambda cut, *refs: wide_sum_kernel(cut, height, slab, *refs)
    )
    field, *around = call(
        part(step_kernel, depth, height), [flat, side, side, plane, plane], [total, *z_pieces, w_low, w_high, *z_pairs]
    )
    g_field, *z_pieces, z_element = call(
        part(z_kernel, depth, height), [flat] + [(depth, height, width)] * 3 + [(7, height, width)], [field, *around]
    )
    total, z_pairs, _ = lines(
        1, None, field, g_field, z_element, z_element, depth, height, height, depth, lambda cut, *refs: sum_kernel(cut, height, *refs)
    )
    rows = slots.shape[0]
    chunks = call(
        part(last_kernel, depth, height),
        [(blocks * size + rows * (k == 0), width) for k, size in enumerate(CHUNKS)],
        [total, *z_pieces, slots, *z_pairs],
    )
    field, incoming = route(chunks, slots, blocks)
    return field.reshape(volume.shape), incoming[None]


def solution(mesh):
    in_specs = (P("gz", "xy", None), P("xy", "gz", None))
    out_specs = (P("gz", "xy", None), P("xy", "gz", None, None))

    return jax.shard_map(on_device, mesh=mesh, in_specs=in_specs, out_specs=out_specs, check_vma=False)
```
